32 devices in a mesh: ctx: 8 (over z, y), fsdp: 4 (over x, core).
Axes of the slice: x: 2, y: 2, z: 4, core: 2. Of those that a mesh axis runs over, the one named last changes fastest.
Arguments:
- tokens: int32 [4096], P('ctx'), may hold values from 0 to 511
- embedding: bfloat16 [512, 4096], P(None, 'fsdp'), may hold values from -6 to 6
- norm_gain: float32 [4096], replicated, may hold values from 0.1 to 1.9
- in_weight: bfloat16 [4096, 3, 2048], P('ctx', None, 'fsdp'), may hold values from -0.09375 to 0.09375
- short_taps: float32 [7, 3, 2048], P(None, None, 'fsdp'), may hold values from -2 to 2
- decay_rates: float32 [16, 128], P(None, 'fsdp'), may hold values from 0.00012207031 to 0.1
- residue: float32 [16, 128], P(None, 'fsdp'), may hold values from -0.15625 to 0.15625
- skip_weight: float32 [2048], P('fsdp'), may hold values from -4 to 4
- out_weight: bfloat16 [2048, 4096], P('fsdp', 'ctx'), may hold values from -0.125 to 0.125
Outputs:
- mixed: bfloat16 [4096, 4096], P('ctx', 'fsdp')
The draws below stay inside these ranges and needn't reach their ends.
All inputs are finite; a program needn't handle non-finite values.
Results may differ from the reference program's by a relative error of at most 0.018.
Values may be sent and summed in bfloat16 or wider, within the bound.
No kernel may reach another device: no remote copies, remote signals or barrier semaphores. Data moves between devices by JAX's collectives and lax.ppermute only.
A program may use at most 64 MiB of HBM per device.

```python
import math
import jax
import jax.numpy as jnp
import numpy as np
from jax import lax

D = 4096
VOCAB = 512
C = 2048
GROUP = 16
MODES = 16
TAPS = 7
SEQ = 4096
GROUPS = 128


def set_ends(drawn, rng, least, largest):
    longest = drawn.shape.index(max(drawn.shape))
    spots = []
    for shift in (0, 1):
        where = [jax.random.randint(jax.random.fold_in(rng, axis), (), 0, length) for axis, length in enumerate(drawn.shape)]
        where[longest] = (where[longest] + shift) % drawn.shape[longest]
        spots.append(tuple(where))
    return drawn.at[spots[0]].set(least).at[spots[1]].set(largest)


def block_scale(stream_key, shape, split, smallest, high):
    level = 1.0
    for axis_at, parts in split:
        heights = jax.random.uniform(jax.random.fold_in(jax.random.fold_in(stream_key, 6), axis_at), (parts,), jnp.float32, smallest / len(split), high / len(split))
        level = level * jnp.repeat(jnp.exp(heights), shape[axis_at] // parts).reshape((-1,) + (1,) * (len(shape) - 1 - axis_at))
    return level


def rank_bounds(number_of, skew):
    loads = [(1 << 20) // math.isqrt(grade ** skew) + 1 for grade in range(1, number_of + 1)]
    scale = 1 + sum(loads) // (1 << 30)
    return np.cumsum(np.array([max(1, weight // scale) for weight in loads]))


def ranked(rng, extent, amount, skew):
    table = rank_bounds(amount, skew)
    pick = jax.random.randint(jax.random.fold_in(rng, 1), extent, 0, int(table[amount - 1]))
    rank = jnp.searchsorted(jnp.asarray(table, jnp.int32), pick, side="right")
    return jax.random.permutation(jax.random.fold_in(rng, 2), amount)[rank].astype(jnp.int32)


def gaussian(stream_key, dims, deviation, most, split=(), kind=jnp.bfloat16):
    level = block_scale(stream_key, dims, split, -0.22, 0.18) if split else 1.0
    result = jax.random.normal(stream_key, dims, jnp.float32) * deviation * level
    return jnp.minimum(jnp.maximum(result, -most), most).astype(kind)


def setup_inputs(seed: int = 0) -> dict:
    seeds = jax.random.split(jax.random.key(seed), 10)
    tokens = set_ends(ranked(seeds[0], (SEQ,), VOCAB, 2), jax.random.fold_in(seeds[0], 3), 0, VOCAB - 1).astype(jnp.int32)
    embedding = gaussian(seeds[1], (VOCAB, D), 1.0, 6.0, ((1, 4),))
    norm_gain = jnp.clip(1.0 + 0.18 * jax.random.normal(seeds[2], (D,), jnp.float32), 0.1, 1.9)
    in_weight = gaussian(seeds[3], (D, 3, C), D ** -0.5, 0.09375, ((0, 8), (2, 4)))
    short_taps = gaussian(seeds[4], (TAPS, 3, C), TAPS ** -0.5, 2.0, ((2, 4),), jnp.float32)
    decay_rates = jnp.clip(jnp.exp(math.log(0.1) - 6.7083283 * jax.random.uniform(seeds[5], (MODES, GROUPS), jnp.float32) ** block_scale(seeds[5], (MODES, GROUPS), ((1, 4),), -0.2, 0.2)), 0.00012207031, 0.1)
    residue = gaussian(seeds[6], (MODES, GROUPS), ((0.5 / SEQ) ** 0.5), 0.15625, ((1, 4),), jnp.float32)
    skip_weight = gaussian(seeds[7], (C,), 1.0, 4.0, ((0, 4),), jnp.float32)
    out_weight = gaussian(seeds[8], (C, D), C ** -0.5, 0.125, ((0, 4), (1, 8)))
    return dict(tokens=tokens, embedding=embedding, norm_gain=norm_gain, in_weight=in_weight, short_taps=short_taps, decay_rates=decay_rates, residue=residue, skip_weight=skip_weight, out_weight=out_weight)


def reference(tokens, embedding, norm_gain, in_weight, short_taps, decay_rates, residue, skip_weight, out_weight):
    features = jnp.take(embedding, tokens, axis=0)
    widened = features.astype(jnp.float32)
    mean_square = lax.optimization_barrier(jnp.mean(widened * widened, axis=1, keepdims=True))
    normed = (widened * lax.rsqrt(mean_square + 1e-05) * norm_gain).astype(jnp.bfloat16)
    projected = jnp.dot(normed, in_weight.reshape(D, 3 * C), preferred_element_type=jnp.float32)
    projected = projected.reshape(SEQ, 3, C).astype(jnp.bfloat16)
    reach_back = TAPS - 1
    extended = jnp.concatenate([jnp.zeros((reach_back, 3, C), jnp.bfloat16), projected], axis=0).astype(jnp.float32)
    short = jnp.zeros((SEQ, 3, C), jnp.float32)
    for lag_step in range(TAPS):
        short = short + short_taps[lag_step] * extended[reach_back - lag_step:reach_back - lag_step + SEQ]
    queries = short[:, 0, :]
    driving = short[:, 1, :] * short[:, 2, :]
    lag_grid = jnp.arange(SEQ, dtype=jnp.float32)
    filters = lax.optimization_barrier(jnp.sum(residue[None, :, :] * jnp.exp(-decay_rates[None, :, :] * lag_grid[:, None, None]), axis=1))
    filter_spec = jnp.fft.rfft(filters, n=2 * SEQ, axis=0)
    drive_spec = jnp.fft.rfft(driving, n=2 * SEQ, axis=0)
    full_spec = jnp.repeat(filter_spec, GROUP, axis=1)
    convolved = jnp.fft.irfft(drive_spec * full_spec, n=2 * SEQ, axis=0)[:SEQ]
    response = convolved + skip_weight * driving
    gated = (queries * response).astype(jnp.bfloat16)
    return jnp.dot(gated, out_weight, preferred_element_type=jnp.float32).astype(jnp.bfloat16)
```

```python
import jax
import jax.numpy as jnp
from jax import lax
from jax.experimental import pallas as pl
from jax.experimental.pallas import tpu as pltpu
from jax.sharding import PartitionSpec as P

GROUP = 16
CHUNK = 256
TILE = 512
AXES = ("ctx", "fsdp")
BF16 = jnp.bfloat16
F32 = jnp.float32


def send(value, ctx_count, fsdp_count, target):
    pairs = []
    for i in range(ctx_count):
        for j in range(fsdp_count):
            to = target(i, j)
            if to is not None:
                pairs.append((i * fsdp_count + j, to[0] * fsdp_count + to[1]))
    return lax.ppermute(value, AXES, pairs)


def split_high_low(value):
    high = value.astype(BF16)
    return high, (value - high.astype(F32)).astype(BF16)


def filter_body(decay_ref, residue_ref, decay_col_ref, residue_col_ref, near_ref, into_ref, outof_ref, step_ref):
    groups, modes = decay_ref.shape
    rows = lax.broadcasted_iota(jnp.int32, (CHUNK, CHUNK), 0)
    cols = lax.broadcasted_iota(jnp.int32, (CHUNK, CHUNK), 1)
    lag = (cols - rows).astype(F32)
    clipped = jnp.maximum(lag, 0.0)
    back = (CHUNK - 1 - lax.broadcasted_iota(jnp.int32, (CHUNK, modes), 0)).astype(F32)
    ahead = (1 + lax.broadcasted_iota(jnp.int32, (modes, CHUNK), 1)).astype(F32)
    for group in range(groups):
        total = jnp.zeros((CHUNK, CHUNK), F32)
        for mode in range(modes):
            total += residue_ref[group, mode] * jnp.exp(-decay_ref[group, mode] * clipped)
        near_ref[group] = jnp.where(lag >= 0.0, total, 0.0).astype(BF16)
        rate_row = decay_col_ref[group, 0:1, :]
        into_high, into_low = split_high_low(jnp.exp(-rate_row * back))
        into_ref[group] = jnp.concatenate([into_high, into_low], axis=1)
        rate_col = jnp.swapaxes(jnp.broadcast_to(rate_row, (8, modes)), 0, 1)[:, 0:1]
        residue_row = residue_col_ref[group, 0:1, :]
        residue_col = jnp.swapaxes(jnp.broadcast_to(residue_row, (8, modes)), 0, 1)[:, 0:1]
        outof_high, outof_low = split_high_low(residue_col * jnp.exp(-rate_col * ahead))
        outof_ref[group] = jnp.concatenate([outof_high, outof_high, outof_low], axis=0)
        step_ref[group] = jnp.exp(-rate_row * CHUNK)


def make_filters(decay, residue):
    groups, modes = decay.shape
    smem = pl.BlockSpec(memory_space=pltpu.SMEM)
    vmem = pl.BlockSpec(memory_space=pltpu.VMEM)
    return pl.pallas_call(
        filter_body,
        in_specs=[smem, smem, vmem, vmem],
        out_specs=[vmem] * 4,
        out_shape=[
            jax.ShapeDtypeStruct((groups, CHUNK, CHUNK), BF16),
            jax.ShapeDtypeStruct((groups, CHUNK, 2 * modes), BF16),
            jax.ShapeDtypeStruct((groups, 3 * modes, CHUNK), BF16),
            jax.ShapeDtypeStruct((groups, 1, modes), F32),
        ],
        name="filters",
    )(decay, residue, decay[:, None, :], residue[:, None, :])


def table_body(low_ref, emb_ref, gain_ref, *refs):
    weight_refs, out_ref = refs[:-1], refs[-1]
    count = len(weight_refs)
    width = emb_ref.shape[1] // count
    pieces, rows, vocab = out_ref.shape
    for kind in range(3):
        total = None
        for shift, weight_ref in enumerate(weight_refs):
            start = pl.multiple_of(lax.rem(low_ref[0] + shift, count) * width, width)
            scaled = (emb_ref[:, pl.ds(start, width)].astype(F32) * gain_ref[:, pl.ds(start, width)]).astype(BF16)
            part = jnp.dot(scaled, weight_ref[kind], preferred_element_type=F32)
            total = part if total is None else total + part
        flipped = jnp.swapaxes(total, 0, 1).astype(BF16)
        each = rows // 3
        for piece in range(pieces):
            out_ref[piece, kind * each:(kind + 1) * each, :] = flipped[piece * each:(piece + 1) * each]


def make_table(low, emb, gain, weights, pieces):
    vocab = emb.shape[0]
    channels = weights[0].shape[2]
    vmem = pl.BlockSpec(memory_space=pltpu.VMEM)
    return pl.pallas_call(
        table_body,
        in_specs=[pl.BlockSpec(memory_space=pltpu.SMEM)] + [vmem] * (2 + len(weights)),
        out_specs=vmem,
        out_shape=jax.ShapeDtypeStruct((pieces, 3 * channels // pieces, vocab), BF16),
        name="table",
    )(low, emb, gain, *weights)


def mixer_body(tokens_ref, scale_ref, taps_ref, skip_ref, near_ref, into_ref, outof_ref, step_ref, *refs):
    piece_refs = refs[:-4]
    out_ref, query_ref, drive_ref, conv_ref = refs[-4:]
    rows, vocab = piece_refs[0].shape
    channels = rows // 3
    length = tokens_ref.shape[1]
    taps = taps_ref.shape[1]
    total = piece_refs[0][...].astype(F32)
    for ref in piece_refs[1:]:
        total += ref[...].astype(F32)
    table = (total * scale_ref[...]).astype(BF16)
    ids = lax.broadcasted_iota(jnp.int32, (vocab, TILE), 0)
    halo = jnp.zeros((rows, 128), F32)
    for tile in range(length // TILE):
        at = tile * TILE
        hot = jnp.where(ids == tokens_ref[:, at:at + TILE], 1.0, 0.0).astype(BF16)
        projected = jnp.dot(table, hot, preferred_element_type=F32)
        extended = jnp.concatenate([halo, projected], axis=1)
        halo = projected[:, TILE - 128:]
        short = taps_ref[:, 0:1] * projected
        for lag in range(1, taps):
            short += taps_ref[:, lag:lag + 1] * pltpu.roll(extended, lag, 1)[:, 128:]
        query_ref[:, at:at + TILE] = short[:channels]
        drive_ref[:, at:at + TILE] = short[channels:2 * channels] * short[2 * channels:]
    groups = near_ref.shape[0]
    per = channels // groups
    modes = step_ref.shape[2]
    chunks = length // CHUNK
    for group in range(groups):
        base = group * per
        stacked = jnp.concatenate(
            [drive_ref[base:base + per, n * CHUNK:(n + 1) * CHUNK] for n in range(chunks)], axis=0
        ).astype(BF16)
        both = jnp.dot(stacked, into_ref[group], preferred_element_type=F32)
        ends = both[:, :modes] + both[:, modes:]
        step = step_ref[group]
        state = jnp.zeros((per, modes), F32)
        starts = []
        for n in range(chunks):
            starts.append(state)
            state = state * step + ends[n * per:(n + 1) * per]
        high, low = split_high_low(jnp.concatenate(starts, axis=0))
        conv_ref[...] = jnp.dot(stacked, near_ref[group], preferred_element_type=F32) + jnp.dot(
            jnp.concatenate([high, low, high], axis=1), outof_ref[group], preferred_element_type=F32
        )
        for n in range(chunks):
            here = slice(n * CHUNK, (n + 1) * CHUNK)
            response = conv_ref[n * per:(n + 1) * per, :] + skip_ref[base:base + per, :] * drive_ref[base:base + per, here]
            out_ref[base:base + per, here] = (query_ref[base:base + per, here] * response).astype(BF16)


def make_mixer(tokens, scale, taps, skip, filters, pieces):
    rows = pieces[0].shape[0]
    channels = rows // 3
    length = tokens.shape[1]
    groups = filters[0].shape[0]
    vmem = pl.BlockSpec(memory_space=pltpu.VMEM)
    return pl.pallas_call(
        mixer_body,
        in_specs=[vmem] * (8 + len(pieces)),
        out_specs=vmem,
        out_shape=jax.ShapeDtypeStruct((channels, length), BF16),
        scratch_shapes=[
            pltpu.VMEM((channels, length), F32),
            pltpu.VMEM((channels, length), F32),
            pltpu.VMEM((length // CHUNK * (channels // groups), CHUNK), F32),
        ],
        name="mixer",
    )(tokens, scale, taps, skip, *filters, *pieces)


def body(
    tokens,
    embedding,
    norm_gain,
    in_weight,
    short_taps,
    decay_rates,
    residue,
    skip_weight,
    out_weight,
):
    ctx_count = lax.axis_size("ctx")
    fsdp_count = lax.axis_size("fsdp")
    lows = ctx_count // fsdp_count
    ctx_at = lax.axis_index("ctx")
    fsdp_at = lax.axis_index("fsdp")
    high_at, low_at = ctx_at // lows, ctx_at % lows
    tok_count = tokens.shape[0]
    vocab, columns = embedding.shape
    local_channels = in_weight.shape[2]
    part = local_channels // lows
    own = local_channels // ctx_count

    def move(value, target):
        return send(value, ctx_count, fsdp_count, target)

    by_kind = jnp.swapaxes(in_weight, 0, 1)
    weights = [lax.dynamic_slice_in_dim(by_kind, low_at * part, part, 2)]
    for shift in range(1, lows):
        going = lax.dynamic_slice_in_dim(by_kind, (low_at - shift) % lows * part, part, 2)
        weights.append(move(going, lambda i, j: (i // lows * lows + (i % lows - shift) % lows, j)))

    half = vocab // 2
    is_source = fsdp_at == high_at
    core_at = fsdp_at % 2
    first, second = embedding[:half], embedding[half:]
    beside = move(embedding, lambda i, j: (i, j ^ 1) if j == i // lows else None)
    arrived_first = jnp.zeros_like(first)
    arrived_second = jnp.zeros_like(second)
    for shift in range(1, fsdp_count // 2):
        def across(core):
            return lambda i, j: (i, (j // 2 + shift) % (fsdp_count // 2) * 2 + core) if j == i // lows else None

        arrived_first = arrived_first + move(first, across(0))
        arrived_second = arrived_second + move(second, across(1))
    swapped = move(
        arrived_first + arrived_second, lambda i, j: (i, j ^ 1) if j // 2 != i // lows // 2 else None
    )
    nothing = jnp.zeros_like(first)
    met = jnp.concatenate(
        [
            jnp.where(is_source, first, beside[:half] + arrived_first + jnp.where(core_at == 1, swapped, nothing)),
            jnp.where(is_source, second, beside[half:] + arrived_second + jnp.where(core_at == 0, swapped, nothing)),
        ],
        axis=0,
    )
    gain = lax.dynamic_slice_in_dim(norm_gain, high_at * columns, columns, 0)[None, :]

    widened = embedding.astype(F32)
    squares = jnp.sum(widened * widened, axis=1)[None, :]
    reach = 1
    while reach < fsdp_count:
        squares = squares + move(squares, lambda i, j: (i, j ^ reach))
        reach *= 2
    scale = lax.rsqrt(squares / (columns * fsdp_count) + 1e-05)

    everywhere = lax.all_gather(tokens, "ctx", axis=0, tiled=True)[None, :]

    moved = move(out_weight, lambda i, j: (j * lows + i % lows, i // lows))
    gathered = lax.all_gather(moved, "ctx", axis=0, tiled=False)

    per_group = min(GROUP, own)
    group_count = own // per_group
    group_at = ctx_place(low_at, high_at, part, own) // GROUP
    decay = lax.dynamic_slice_in_dim(decay_rates.T, group_at, group_count, 0)
    weight = lax.dynamic_slice_in_dim(residue.T, group_at, group_count, 0)
    filters = make_filters(decay, weight)
    channel_at = ctx_place(low_at, high_at, part, own)
    taps = lax.dynamic_slice_in_dim(short_taps, channel_at, own, 2)
    taps = taps.reshape(taps.shape[0], 3 * own).T
    skip = lax.dynamic_slice_in_dim(skip_weight, channel_at, own, 0)[:, None]

    partial = make_table(low_at[None], met, gain, weights, fsdp_count)
    pieces = [lax.dynamic_index_in_dim(partial, high_at, 0, keepdims=False)]
    for shift in range(1, fsdp_count):
        going = lax.dynamic_index_in_dim(partial, (high_at + shift) % fsdp_count, 0, keepdims=False)
        pieces.append(move(going, lambda i, j: ((i // lows + shift) % fsdp_count * lows + i % lows, j)))

    gated = make_mixer(everywhere, scale, taps, skip, filters, pieces)

    blocks = [lax.dynamic_slice_in_dim(gated, ctx_at * tok_count, tok_count, 1)]
    for shift in range(1, ctx_count):
        going = lax.dynamic_slice_in_dim(gated, (ctx_at + shift) % ctx_count * tok_count, tok_count, 1)
        blocks.append(move(going, lambda i, j: ((i + shift) % ctx_count, j)))
    ordered = jnp.stack(blocks[::-1], axis=0)
    ordered = jnp.roll(ordered, ctx_at + 1, axis=0)
    ordered = ordered.reshape(fsdp_count, lows, own, tok_count).swapaxes(0, 1).reshape(local_channels, tok_count)
    sides = [ordered]
    result = None
    order = [0]
    reach = 1
    while reach < fsdp_count:
        more = [move(side, lambda i, j: (i, j ^ reach)) for side in sides]
        sides, order = sides + more, order + [at ^ reach for at in order]
        reach *= 2
    for flip, side in zip(order, sides):
        rows_at = fsdp_at ^ flip
        wide = lax.dynamic_slice_in_dim(gathered, rows_at * lows, lows, 0)
        wide = wide.swapaxes(0, 1).reshape(local_channels, lows * out_weight.shape[1])
        term = lax.dot_general(side, wide, (((0,), (0,)), ((), ())), preferred_element_type=F32)
        result = term if result is None else result + term
    return result.astype(BF16)


def ctx_place(low_at, high_at, part, own):
    return low_at * part + high_at * own


def solution(mesh):
    placed = (
        P("ctx"),
        P(None, "fsdp"),
        P(),
        P("ctx", None, "fsdp"),
        P(None, None, "fsdp"),
        P(None, "fsdp"),
        P(None, "fsdp"),
        P("fsdp"),
        P("fsdp", "ctx"),
    )
    return jax.shard_map(
        body, mesh=mesh, in_specs=placed, out_specs=P("ctx", "fsdp"), check_vma=False
    )
```

```python
import jax
import jax.numpy as jnp
from jax import lax
from jax.experimental import pallas as pl
from jax.experimental.pallas import tpu as pltpu
from jax.sharding import PartitionSpec as P

GROUP = 16
CHUNK = 256
TILE = 512
AXES = ("ctx", "fsdp")
BF16 = jnp.bfloat16
F32 = jnp.float32


def send(value, ctx_count, fsdp_count, target):
    pairs = []
    for i in range(ctx_count):
        for j in range(fsdp_count):
            to = target(i, j)
            if to is not None:
                pairs.append((i * fsdp_count + j, to[0] * fsdp_count + to[1]))
    return lax.ppermute(value, AXES, pairs)


def split_high_low(value):
    high = value.astype(BF16)
    return high, (value - high.astype(F32)).astype(BF16)


def filter_body(decay_ref, residue_ref, decay_col_ref, residue_col_ref, near_ref, into_ref, outof_ref, step_ref):
    groups, modes = decay_ref.shape
    rows = lax.broadcasted_iota(jnp.int32, (CHUNK, CHUNK), 0)
    cols = lax.broadcasted_iota(jnp.int32, (CHUNK, CHUNK), 1)
    lag = (cols - rows).astype(F32)
    clipped = jnp.maximum(lag, 0.0)
    back = (CHUNK - 1 - lax.broadcasted_iota(jnp.int32, (CHUNK, modes), 0)).astype(F32)
    ahead = (1 + lax.broadcasted_iota(jnp.int32, (modes, CHUNK), 1)).astype(F32)
    for group in range(groups):
        total = jnp.zeros((CHUNK, CHUNK), F32)
        for mode in range(modes):
            total += residue_ref[group, mode] * jnp.exp(-decay_ref[group, mode] * clipped)
        near_ref[group] = jnp.where(lag >= 0.0, total, 0.0).astype(BF16)
        rate_row = decay_col_ref[group, 0:1, :]
        into_high, into_low = split_high_low(jnp.exp(-rate_row * back))
        into_ref[group] = jnp.concatenate([into_high, into_low], axis=1)
        rate_col = jnp.swapaxes(jnp.broadcast_to(rate_row, (8, modes)), 0, 1)[:, 0:1]
        residue_row = residue_col_ref[group, 0:1, :]
        residue_col = jnp.swapaxes(jnp.broadcast_to(residue_row, (8, modes)), 0, 1)[:, 0:1]
        outof_high, outof_low = split_high_low(residue_col * jnp.exp(-rate_col * ahead))
        outof_ref[group] = jnp.concatenate([outof_high, outof_high, outof_low], axis=0)
        step_ref[group] = jnp.exp(-rate_row * CHUNK)


def make_filters(decay, residue):
    groups, modes = decay.shape
    smem = pl.BlockSpec(memory_space=pltpu.SMEM)
    vmem = pl.BlockSpec(memory_space=pltpu.VMEM)
    return pl.pallas_call(
        filter_body,
        in_specs=[smem, smem, vmem, vmem],
        out_specs=[vmem] * 4,
        out_shape=[
            jax.ShapeDtypeStruct((groups, CHUNK, CHUNK), BF16),
            jax.ShapeDtypeStruct((groups, CHUNK, 2 * modes), BF16),
            jax.ShapeDtypeStruct((groups, 3 * modes, CHUNK), BF16),
            jax.ShapeDtypeStruct((groups, 1, modes), F32),
        ],
        name="filters",
    )(decay, residue, decay[:, None, :], residue[:, None, :])


def table_body(place_ref, own_ref, beside_ref, arrived_ref, swapped_ref, gain_ref, *refs):
    weight_refs, out_ref, scaled_ref = refs[:-2], refs[-2], refs[-1]
    count = len(weight_refs)
    vocab, columns = own_ref.shape
    half = vocab // 2
    width = columns // count
    pieces, rows, _ = out_ref.shape
    low_at, is_source, is_beside, core_at = place_ref[0], place_ref[1], place_ref[2], place_ref[3]

    @pl.when(is_source == 1)
    def _():
        scaled_ref[...] = (own_ref[...].astype(F32) * gain_ref[...]).astype(BF16)

    @pl.when(is_beside == 1)
    def _():
        scaled_ref[...] = (beside_ref[...].astype(F32) * gain_ref[...]).astype(BF16)

    @pl.when(jnp.logical_and(is_source == 0, is_beside == 0))
    def _():
        near = pl.multiple_of(core_at * half, half)
        far = pl.multiple_of((1 - core_at) * half, half)
        scaled_ref[pl.ds(near, half), :] = (arrived_ref[...].astype(F32) * gain_ref[...]).astype(BF16)
        scaled_ref[pl.ds(far, half), :] = (swapped_ref[...].astype(F32) * gain_ref[...]).astype(BF16)

    each = rows // 3
    for kind in range(3):
        total = None
        for shift, weight_ref in enumerate(weight_refs):
            start = pl.multiple_of(lax.rem(low_at + shift, count) * width, width)
            part = jnp.dot(scaled_ref[:, pl.ds(start, width)], weight_ref[kind], preferred_element_type=F32)
            total = part if total is None else total + part
        flipped = jnp.swapaxes(total, 0, 1).astype(BF16)
        for piece in range(pieces):
            out_ref[piece, kind * each:(kind + 1) * each, :] = flipped[piece * each:(piece + 1) * each]


def make_table(place, own, beside, arrived, swapped, gain, weights, pieces):
    vocab = own.shape[0]
    channels = weights[0].shape[2]
    vmem = pl.BlockSpec(memory_space=pltpu.VMEM)
    return pl.pallas_call(
        table_body,
        in_specs=[pl.BlockSpec(memory_space=pltpu.SMEM)] + [vmem] * (5 + len(weights)),
        out_specs=vmem,
        out_shape=jax.ShapeDtypeStruct((pieces, 3 * channels // pieces, vocab), BF16),
        scratch_shapes=[pltpu.VMEM(own.shape, BF16)],
        name="table",
    )(place, own, beside, arrived, swapped, gain, *weights)


def mixer_body(place_ref, tokens_ref, scale_ref, taps_ref, skip_ref, near_ref, into_ref, outof_ref, step_ref, *refs):
    piece_refs = refs[:-4]
    out_ref, query_ref, drive_ref, conv_ref = refs[-4:]
    rows, vocab = piece_refs[0].shape
    channels = rows // 3
    blocks, _, block = tokens_ref.shape
    length = blocks * block
    taps = taps_ref.shape[1]
    total = piece_refs[0][...].astype(F32)
    for ref in piece_refs[1:]:
        total += ref[...].astype(F32)
    table = (total * scale_ref[...]).astype(BF16)
    ids = lax.broadcasted_iota(jnp.int32, (vocab, TILE), 0)
    halo = jnp.zeros((rows, 128), F32)
    for tile in range(length // TILE):
        at = tile * TILE
        inside = at % block
        tokens = tokens_ref[at // block ^ place_ref[0]][:, inside:inside + TILE]
        hot = jnp.where(ids == tokens, 1.0, 0.0).astype(BF16)
        projected = jnp.dot(table, hot, preferred_element_type=F32)
        extended = jnp.concatenate([halo, projected], axis=1)
        halo = projected[:, TILE - 128:]
        short = taps_ref[:, 0:1] * projected
        for lag in range(1, taps):
            short += taps_ref[:, lag:lag + 1] * pltpu.roll(extended, lag, 1)[:, 128:]
        query_ref[:, at:at + TILE] = short[:channels]
        drive_ref[:, at:at + TILE] = short[channels:2 * channels] * short[2 * channels:]
    groups = near_ref.shape[0]
    per = channels // groups
    modes = step_ref.shape[2]
    chunks = length // CHUNK
    for group in range(groups):
        base = group * per
        stacked = jnp.concatenate(
            [drive_ref[base:base + per, n * CHUNK:(n + 1) * CHUNK] for n in range(chunks)], axis=0
        ).astype(BF16)
        both = jnp.dot(stacked, into_ref[group], preferred_element_type=F32)
        ends = both[:, :modes] + both[:, modes:]
        step = step_ref[group]
        state = jnp.zeros((per, modes), F32)
        starts = []
        for n in range(chunks):
            starts.append(state)
            state = state * step + ends[n * per:(n + 1) * per]
        high, low = split_high_low(jnp.concatenate(starts, axis=0))
        conv_ref[...] = jnp.dot(stacked, near_ref[group], preferred_element_type=F32) + jnp.dot(
            jnp.concatenate([high, low, high], axis=1), outof_ref[group], preferred_element_type=F32
        )
        for n in range(chunks):
            here = slice(n * CHUNK, (n + 1) * CHUNK)
            response = conv_ref[n * per:(n + 1) * per, :] + skip_ref[base:base + per, :] * drive_ref[base:base + per, here]
            out_ref[base:base + per, here] = (query_ref[base:base + per, here] * response).astype(BF16)


def make_mixer(place, tokens, scale, taps, skip, filters, pieces):
    rows = pieces[0].shape[0]
    channels = rows // 3
    length = tokens.shape[0] * tokens.shape[2]
    groups = filters[0].shape[0]
    vmem = pl.BlockSpec(memory_space=pltpu.VMEM)
    return pl.pallas_call(
        mixer_body,
        in_specs=[pl.BlockSpec(memory_space=pltpu.SMEM)] + [vmem] * (8 + len(pieces)),
        out_specs=vmem,
        out_shape=jax.ShapeDtypeStruct((channels, length), BF16),
        scratch_shapes=[
            pltpu.VMEM((channels, length), F32),
            pltpu.VMEM((channels, length), F32),
            pltpu.VMEM((length // CHUNK * (channels // groups), CHUNK), F32),
        ],
        name="mixer",
    )(place, tokens, scale, taps, skip, *filters, *pieces)


def order_body(place_ref, *refs):
    piece_refs, out_ref, stage_ref = refs[:-2], refs[-2], refs[-1]
    count = len(piece_refs)
    rows = piece_refs[0].shape[0]
    lows = place_ref[1]
    for shift, ref in enumerate(piece_refs):
        source = lax.rem(place_ref[0] - shift + count, count)
        start = pl.multiple_of((lax.rem(source, lows) * (count // lows) + source // lows) * rows, rows)
        stage_ref[pl.ds(start, rows), :] = ref[...].astype(F32)
    out_ref[...] = jnp.swapaxes(stage_ref[...], 0, 1).astype(BF16)


def make_order(place, pieces):
    rows, length = pieces[0].shape
    vmem = pl.BlockSpec(memory_space=pltpu.VMEM)
    return pl.pallas_call(
        order_body,
        in_specs=[pl.BlockSpec(memory_space=pltpu.SMEM)] + [vmem] * len(pieces),
        out_specs=vmem,
        out_shape=jax.ShapeDtypeStruct((length, rows * len(pieces)), BF16),
        scratch_shapes=[pltpu.VMEM((rows * len(pieces), length), F32)],
        name="order",
    )(place, *pieces)


def arrange_body(rows_ref, lows_ref, *refs):
    block_refs, out_ref = refs[:-1], refs[-1]
    full, cols = block_refs[0].shape
    for at, ref in enumerate(block_refs):
        start = pl.multiple_of(lows_ref[at] * cols, cols)
        first = 0 if ref.shape[0] == full or at == len(block_refs) - 2 else full // 2
        out_ref[rows_ref[at], first:first + ref.shape[0], pl.ds(start, cols)] = ref[...]


def make_arrange(rows_at, lows_at, blocks, sides, lows):
    full, cols = blocks[0].shape
    smem = pl.BlockSpec(memory_space=pltpu.SMEM)
    vmem = pl.BlockSpec(memory_space=pltpu.VMEM)
    return pl.pallas_call(
        arrange_body,
        in_specs=[smem, smem] + [vmem] * len(blocks),
        out_specs=vmem,
        out_shape=jax.ShapeDtypeStruct((sides, full, lows * cols), BF16),
        name="arrange",
    )(rows_at, lows_at, *blocks)


def product_body(at_ref, wide_ref, *refs):
    side_refs, out_ref = refs[:-1], refs[-1]
    total = None
    if side_refs[0].dtype == F32:
        total, side_refs = side_refs[0][...], side_refs[1:]
    for index, ref in enumerate(side_refs):
        term = jnp.dot(ref[...], wide_ref[at_ref[index]], preferred_element_type=F32)
        total = term if total is None else total + term
    out_ref[...] = total.astype(out_ref.dtype)


def make_product(at, wide, sides, kind):
    smem = pl.BlockSpec(memory_space=pltpu.SMEM)
    vmem = pl.BlockSpec(memory_space=pltpu.VMEM)
    return pl.pallas_call(
        product_body,
        in_specs=[smem, vmem] + [vmem] * len(sides),
        out_specs=vmem,
        out_shape=jax.ShapeDtypeStruct((sides[-1].shape[0], wide.shape[2]), kind),
        name="product",
    )(at, wide, *sides)


def reverse_bits(value, count):
    result = 0
    while count > 1:
        result, value, count = result * 2 + value % 2, value // 2, count // 2
    return result


def cycle_of(highs, lows):
    walk = [(high, 0) for high in range(highs)]
    for at in range(highs - 1, -1, -1):
        lows_at = range(1, lows) if (highs - 1 - at) % 2 == 0 else range(lows - 1, 0, -1)
        walk += [(at, low) for low in lows_at]
    return [high * lows + low for high, low in walk]


def body(
    tokens,
    embedding,
    norm_gain,
    in_weight,
    short_taps,
    decay_rates,
    residue,
    skip_weight,
    out_weight,
):
    ctx_count = lax.axis_size("ctx")
    fsdp_count = lax.axis_size("fsdp")
    lows = ctx_count // fsdp_count
    ctx_at = lax.axis_index("ctx")
    fsdp_at = lax.axis_index("fsdp")
    high_at, low_at = ctx_at // lows, ctx_at % lows
    tok_count = tokens.shape[0]
    vocab, columns = embedding.shape
    local_channels = in_weight.shape[2]
    part = local_channels // lows
    own = local_channels // ctx_count

    def move(value, target):
        return send(value, ctx_count, fsdp_count, target)

    by_kind = jnp.swapaxes(in_weight, 0, 1)
    weights = [lax.dynamic_slice_in_dim(by_kind, low_at * part, part, 2)]
    for shift in range(1, lows):
        going = lax.dynamic_slice_in_dim(by_kind, (low_at - shift) % lows * part, part, 2)
        weights.append(move(going, lambda i, j: (i // lows * lows + (i % lows - shift) % lows, j)))

    half = vocab // 2
    chips = fsdp_count // 2
    core_at = fsdp_at % 2
    arrived = None
    for shift in range(1, chips):
        for core, part_of in enumerate((embedding[:half], embedding[half:])):
            got = move(
                part_of,
                lambda i, j: (i, (j // 2 + shift) % chips * 2 + core) if j == i // lows else None,
            )
            arrived = got if arrived is None else arrived + got
    beside = move(embedding, lambda i, j: (i, j ^ 1) if j == i // lows else None)
    swapped = move(arrived, lambda i, j: (i, j ^ 1) if j // 2 != i // lows // 2 else None)
    gain = lax.dynamic_slice_in_dim(norm_gain, high_at * columns, columns, 0)[None, :]

    widened = embedding.astype(F32)
    squares = jnp.sum(widened * widened, axis=1)[None, :]
    reach = 1
    while reach < fsdp_count:
        squares = squares + move(squares, lambda i, j: (i, j ^ reach))
        reach *= 2
    scale = lax.rsqrt(squares / (columns * fsdp_count) + 1e-05)

    everywhere = tokens[None, None, :]
    reach = 1
    while reach < ctx_count:
        everywhere = jnp.concatenate([everywhere, move(everywhere, lambda i, j: (i ^ reach, j))], axis=0)
        reach *= 2

    cycle = cycle_of(fsdp_count, lows)
    spot = {ctx: at for at, ctx in enumerate(cycle)}
    moved = move(
        out_weight,
        lambda i, j: ((reverse_bits(j, fsdp_count) ^ i // lows) * lows + i % lows, i // lows),
    )
    ahead, behind = [moved], [moved]
    for _ in range((ctx_count - 1) // 2):
        ahead.append(move(ahead[-1], lambda i, j: (cycle[(spot[i] + 1) % ctx_count], j)))
        behind.append(move(behind[-1], lambda i, j: (cycle[(spot[i] - 1) % ctx_count], j)))
    middle = out_weight.shape[0] // 2
    last_ahead = move(ahead[-1][:middle], lambda i, j: (cycle[(spot[i] + 1) % ctx_count], j))
    last_behind = move(behind[-1][middle:], lambda i, j: (cycle[(spot[i] - 1) % ctx_count], j))
    blocks = ahead + behind[1:] + [last_ahead, last_behind]
    steps = list(range(len(ahead))) + [-at for at in range(1, len(behind))] + [len(ahead)] * 2
    spots = jnp.array([spot[ctx] for ctx in range(ctx_count)], jnp.int32)
    sources = jnp.array(cycle, jnp.int32)[(spots[ctx_at] - jnp.array(steps, jnp.int32)) % ctx_count]
    reversed_bits = jnp.array([reverse_bits(at, fsdp_count) for at in range(fsdp_count)], jnp.int32)
    wide = make_arrange(
        reversed_bits[sources // lows ^ fsdp_at], sources % lows, blocks, fsdp_count, lows
    )

    channel_at = low_at * part + high_at * own
    per_group = min(GROUP, own)
    group_count = own // per_group
    decay = lax.dynamic_slice_in_dim(decay_rates.T, channel_at // GROUP, group_count, 0)
    weight = lax.dynamic_slice_in_dim(residue.T, channel_at // GROUP, group_count, 0)
    filters = make_filters(decay, weight)
    taps = lax.dynamic_slice_in_dim(short_taps, channel_at, own, 2)
    taps = taps.reshape(taps.shape[0], 3 * own).T
    skip = lax.dynamic_slice_in_dim(skip_weight, channel_at, own, 0)[:, None]

    place = jnp.stack([
        low_at,
        (fsdp_at == high_at).astype(jnp.int32),
        (fsdp_at == high_at ^ 1).astype(jnp.int32),
        core_at,
    ])
    partial = make_table(place, embedding, beside, arrived, swapped, gain, weights, fsdp_count)
    pieces = [lax.dynamic_index_in_dim(partial, high_at, 0, keepdims=False)]
    for shift in range(1, fsdp_count):
        going = lax.dynamic_index_in_dim(partial, (high_at + shift) % fsdp_count, 0, keepdims=False)
        pieces.append(move(going, lambda i, j: ((i // lows + shift) % fsdp_count * lows + i % lows, j)))

    ctx_place = jnp.stack([ctx_at, jnp.int32(lows)])
    gated = make_mixer(ctx_place, everywhere, scale, taps, skip, filters, pieces)

    pieces = [lax.dynamic_slice_in_dim(gated, ctx_at * tok_count, tok_count, 1)]
    for shift in range(1, ctx_count):
        going = lax.dynamic_slice_in_dim(gated, (ctx_at + shift) % ctx_count * tok_count, tok_count, 1)
        pieces.append(move(going, lambda i, j: ((i + shift) % ctx_count, j)))
    ordered = make_order(ctx_place, pieces)
    sides, order = [ordered], [0]
    reach = fsdp_count // 2
    while reach:
        sides = sides + [move(side, lambda i, j: (i, j ^ reach)) for side in sides]
        order = order + [at ^ reach for at in order]
        reach //= 2
    at = jnp.array(order, jnp.int32) ^ fsdp_at
    return make_product(at, wide, sides, BF16)


def solution(mesh):
    placed = (
        P("ctx"),
        P(None, "fsdp"),
        P(),
        P("ctx", None, "fsdp"),
        P(None, None, "fsdp"),
        P(None, "fsdp"),
        P(None, "fsdp"),
        P("fsdp"),
        P("fsdp", "ctx"),
    )
    return jax.shard_map(
        body, mesh=mesh, in_specs=placed, out_specs=P("ctx", "fsdp"), check_vma=False
    )
```

```python
import functools

import jax
import jax.numpy as jnp
from jax import lax
from jax.experimental import pallas as pl
from jax.experimental.pallas import tpu as pltpu
from jax.sharding import PartitionSpec as P


GROUP = 16
CHUNK = 256
TILE = 512
EXTRA = 16
BASE = 16
AXES = ("ctx", "fsdp")
BF16 = jnp.bfloat16
F32 = jnp.float32


def send(value, ctx_count, fsdp_count, target):
    pairs = []
    for i in range(ctx_count):
        for j in range(fsdp_count):
            to = target(i, j)
            if to is not None:
                pairs.append((i * fsdp_count + j, to[0] * fsdp_count + to[1]))
    return lax.ppermute(value, AXES, pairs)


def after(values, *others):
    return lax.optimization_barrier((tuple(values), others))[0]


def split_high_low(value):
    high = value.astype(BF16)
    return high, (value - high.astype(F32)).astype(BF16)


def filter_body(decay_ref, residue_ref, decay_col_ref, residue_col_ref, near_ref, into_ref, outof_ref, step_ref):
    groups, modes = decay_ref.shape
    rows = lax.broadcasted_iota(jnp.int32, (CHUNK, CHUNK), 0)
    cols = lax.broadcasted_iota(jnp.int32, (CHUNK, CHUNK), 1)
    lag = (cols - rows).astype(F32)
    clipped = jnp.maximum(lag, 0.0)
    back = (CHUNK - 1 - lax.broadcasted_iota(jnp.int32, (CHUNK, modes), 0)).astype(F32)
    ahead = (1 + lax.broadcasted_iota(jnp.int32, (modes, CHUNK), 1)).astype(F32)
    for group in range(groups):
        total = jnp.zeros((CHUNK, CHUNK), F32)
        for mode in range(modes):
            total += residue_ref[group, mode] * jnp.exp(-decay_ref[group, mode] * clipped)
        near_ref[group] = jnp.where(lag >= 0.0, total, 0.0).astype(BF16)
        rate_row = decay_col_ref[group, 0:1, :]
        into_high, into_low = split_high_low(jnp.exp(-rate_row * back))
        into_ref[group] = jnp.concatenate([into_high, into_low], axis=1)
        rate_col = jnp.swapaxes(jnp.broadcast_to(rate_row, (8, modes)), 0, 1)[:, 0:1]
        residue_row = residue_col_ref[group, 0:1, :]
        residue_col = jnp.swapaxes(jnp.broadcast_to(residue_row, (8, modes)), 0, 1)[:, 0:1]
        outof_high, outof_low = split_high_low(residue_col * jnp.exp(-rate_col * ahead))
        outof_ref[group] = jnp.concatenate([outof_high, outof_high, outof_low], axis=0)
        step_ref[group] = jnp.exp(-rate_row * CHUNK)


def make_filters(decay, residue):
    groups, modes = decay.shape
    smem = pl.BlockSpec(memory_space=pltpu.SMEM)
    vmem = pl.BlockSpec(memory_space=pltpu.VMEM)
    return pl.pallas_call(
        filter_body,
        in_specs=[smem, smem, vmem, vmem],
        out_specs=[vmem] * 4,
        out_shape=[
            jax.ShapeDtypeStruct((groups, CHUNK, CHUNK), BF16),
            jax.ShapeDtypeStruct((groups, CHUNK, 2 * modes), BF16),
            jax.ShapeDtypeStruct((groups, 3 * modes, CHUNK), BF16),
            jax.ShapeDtypeStruct((groups, 1, modes), F32),
        ],
        name="filters",
    )(decay, residue, decay[:, None, :], residue[:, None, :])


def table_body(place_ref, own_ref, across_ref, beside_ref, gain_ref, *refs):
    out_ref, raw_ref, scaled_ref, extra_ref = refs[-4:]
    count = (len(refs) - 4) // 2
    weight_refs, token_refs = refs[:count], refs[count:2 * count]
    vocab, columns = own_ref.shape
    width = columns // count
    pieces, rows, _ = out_ref.shape
    low_at, origin = place_ref[0], place_ref[1]

    @pl.when(origin == 0)
    def _():
        raw_ref[...] = own_ref[...].astype(F32)

    @pl.when(origin == 1)
    def _():
        raw_ref[...] = across_ref[...].astype(F32)

    @pl.when(origin == 2)
    def _():
        raw_ref[...] = beside_ref[...].astype(F32)

    raw = raw_ref[...]
    scaled_ref[...] = (raw * gain_ref[...]).astype(BF16)
    extra_ref[...] = jnp.zeros_like(extra_ref)
    squares = jnp.broadcast_to(jnp.sum(raw * raw, axis=1, keepdims=True), (vocab, 128))
    squares = jnp.swapaxes(squares, 0, 1)[0:1, :]
    for row in range(3):
        rounded = squares.astype(BF16).astype(F32)
        extra_ref[row:row + 1, :] = rounded
        squares = squares - rounded
    for shift, token_ref in enumerate(token_refs):
        low = lax.rem(low_at + shift, count)
        extra_ref[pl.ds(3 + low, 1), :] = (token_ref[...] // BASE).astype(F32)
        extra_ref[pl.ds(3 + count + low, 1), :] = (token_ref[...] % BASE).astype(F32)
    extra = extra_ref[...].astype(BF16)
    each = (rows - EXTRA) // 3
    for piece in range(pieces):
        out_ref[piece, :EXTRA, :] = extra
    for kind in range(3):
        total = None
        for shift, weight_ref in enumerate(weight_refs):
            start = pl.multiple_of(lax.rem(low_at + shift, count) * width, width)
            part = jnp.dot(scaled_ref[:, pl.ds(start, width)], weight_ref[kind], preferred_element_type=F32)
            total = part if total is None else total + part
        flipped = jnp.swapaxes(total, 0, 1).astype(BF16)
        for piece in range(pieces):
            out_ref[piece, EXTRA + kind * each:EXTRA + (kind + 1) * each, :] = flipped[piece * each:(piece + 1) * each]


def make_table(place, own, across, beside, gain, weights, tokens, pieces):
    vocab = own.shape[0]
    channels = weights[0].shape[2]
    vmem = pl.BlockSpec(memory_space=pltpu.VMEM)
    return pl.pallas_call(
        table_body,
        in_specs=[pl.BlockSpec(memory_space=pltpu.SMEM)] + [vmem] * (4 + len(weights) + len(tokens)),
        out_specs=vmem,
        out_shape=jax.ShapeDtypeStruct((pieces, EXTRA + 3 * channels // pieces, vocab), BF16),
        scratch_shapes=[
            pltpu.VMEM(own.shape, F32),
            pltpu.VMEM(own.shape, BF16),
            pltpu.VMEM((EXTRA, vocab), F32),
        ],
        name="table",
    )(place, own, across, beside, gain, *weights, *tokens)


def mixer_body(width, place_ref, taps_ref, skip_ref, near_ref, into_ref, outof_ref, step_ref, *refs):
    piece_refs = refs[:-5]
    out_ref, query_ref, drive_ref, conv_ref, token_ref = refs[-5:]
    rows, vocab = piece_refs[0].shape
    rows -= EXTRA
    channels = rows // 3
    blocks, _, block = token_ref.shape
    length = blocks * block
    count = len(piece_refs)
    lows = blocks // count
    taps = taps_ref.shape[1]
    total = None
    squares = None
    for shift, ref in enumerate(piece_refs):
        head = ref[:EXTRA, :].astype(F32)
        summed = head[0:1] + head[1:2] + head[2:3]
        squares = summed if squares is None else squares + summed
        high = lax.rem(place_ref[0] // lows - shift + count, count)
        for low in range(lows):
            ids = head[3 + low:4 + low] * BASE + head[3 + lows + low:4 + lows + low]
            token_ref[high * lows + low] = ids[:, :block].astype(jnp.int32)
        part = ref[EXTRA:, :].astype(F32)
        total = part if total is None else total + part
    table = (total * lax.rsqrt(squares * (1.0 / width) + 1e-05)).astype(BF16)
    ids = lax.broadcasted_iota(jnp.int32, (vocab, TILE), 0)
    halo = jnp.zeros((rows, 128), F32)
    for tile in range(length // TILE):
        at = tile * TILE
        inside = at % block
        tokens = token_ref[at // block][:, inside:inside + TILE]
        hot = jnp.where(ids == tokens, 1.0, 0.0).astype(BF16)
        projected = jnp.dot(table, hot, preferred_element_type=F32)
        extended = jnp.concatenate([halo, projected], axis=1)
        halo = projected[:, TILE - 128:]
        short = taps_ref[:, 0:1] * projected
        for lag in range(1, taps):
            short += taps_ref[:, lag:lag + 1] * pltpu.roll(extended, lag, 1)[:, 128:]
        query_ref[:, at:at + TILE] = short[:channels]
        drive_ref[:, at:at + TILE] = short[channels:2 * channels] * short[2 * channels:]
    groups = near_ref.shape[0]
    per = channels // groups
    modes = step_ref.shape[2]
    chunks = length // CHUNK
    for group in range(groups):
        base = group * per
        stacked = jnp.concatenate(
            [drive_ref[base:base + per, n * CHUNK:(n + 1) * CHUNK] for n in range(chunks)], axis=0
        ).astype(BF16)
        both = jnp.dot(stacked, into_ref[group], preferred_element_type=F32)
        ends = both[:, :modes] + both[:, modes:]
        step = step_ref[group]
        state = jnp.zeros((per, modes), F32)
        starts = []
        for n in range(chunks):
            starts.append(state)
            state = state * step + ends[n * per:(n + 1) * per]
        high, low = split_high_low(jnp.concatenate(starts, axis=0))
        conv_ref[...] = jnp.dot(stacked, near_ref[group], preferred_element_type=F32) + jnp.dot(
            jnp.concatenate([high, low, high], axis=1), outof_ref[group], preferred_element_type=F32
        )
        for n in range(chunks):
            here = slice(n * CHUNK, (n + 1) * CHUNK)
            response = conv_ref[n * per:(n + 1) * per, :] + skip_ref[base:base + per, :] * drive_ref[base:base + per, here]
            out_ref[base:base + per, here] = (query_ref[base:base + per, here] * response).astype(BF16)


def make_mixer(place, width, block, taps, skip, filters, pieces, blocks):
    rows = pieces[0].shape[0] - EXTRA
    channels = rows // 3
    length = block * blocks
    groups = filters[0].shape[0]
    vmem = pl.BlockSpec(memory_space=pltpu.VMEM)
    return pl.pallas_call(
        functools.partial(mixer_body, width),
        in_specs=[pl.BlockSpec(memory_space=pltpu.SMEM)] + [vmem] * (6 + len(pieces)),
        out_specs=vmem,
        out_shape=jax.ShapeDtypeStruct((channels, length), BF16),
        scratch_shapes=[
            pltpu.VMEM((channels, length), F32),
            pltpu.VMEM((channels, length), F32),
            pltpu.VMEM((length // CHUNK * (channels // groups), CHUNK), F32),
            pltpu.VMEM((blocks, 1, block), jnp.int32),
        ],
        name="mixer",
    )(place, taps, skip, *filters, *pieces)


def order_body(place_ref, *refs):
    piece_refs, out_ref, stage_ref = refs[:-2], refs[-2], refs[-1]
    count = len(piece_refs)
    rows = piece_refs[0].shape[0]
    lows = place_ref[1]
    for shift, ref in enumerate(piece_refs):
        source = lax.rem(place_ref[0] - shift + count, count)
        start = pl.multiple_of((lax.rem(source, lows) * (count // lows) + source // lows) * rows, rows)
        stage_ref[pl.ds(start, rows), :] = ref[...].astype(F32)
    out_ref[...] = jnp.swapaxes(stage_ref[...], 0, 1).astype(BF16)


def make_order(place, pieces):
    rows, length = pieces[0].shape
    vmem = pl.BlockSpec(memory_space=pltpu.VMEM)
    return pl.pallas_call(
        order_body,
        in_specs=[pl.BlockSpec(memory_space=pltpu.SMEM)] + [vmem] * len(pieces),
        out_specs=vmem,
        out_shape=jax.ShapeDtypeStruct((length, rows * len(pieces)), BF16),
        scratch_shapes=[pltpu.VMEM((rows * len(pieces), length), F32)],
        name="order",
    )(place, *pieces)


def product_body(order, flips_ref, lows_ref, *refs):
    side_refs = refs[:len(order)]
    block_refs = refs[len(order):-3]
    out_ref, sides_ref, sum_ref = refs[-3:]
    for flip, ref in zip(order, side_refs):
        sides_ref[flip] = ref[...]
    full, cols = block_refs[0].shape
    sum_ref[...] = jnp.zeros_like(sum_ref)
    for at, ref in enumerate(block_refs):
        first = full // 2 if at == len(block_refs) - 1 else 0
        side = sides_ref[flips_ref[at], :, first:first + ref.shape[0]]
        sum_ref[lows_ref[at]] += jnp.dot(side, ref[...], preferred_element_type=F32)
    for low in range(sum_ref.shape[0]):
        out_ref[:, low * cols:(low + 1) * cols] = sum_ref[low].astype(BF16)


def make_product(flips, lows_at, order, sides, blocks, lows):
    length, full = sides[0].shape
    cols = blocks[0].shape[1]
    smem = pl.BlockSpec(memory_space=pltpu.SMEM)
    vmem = pl.BlockSpec(memory_space=pltpu.VMEM)
    return pl.pallas_call(
        functools.partial(product_body, order),
        in_specs=[smem, smem] + [vmem] * (len(sides) + len(blocks)),
        out_specs=vmem,
        out_shape=jax.ShapeDtypeStruct((length, lows * cols), BF16),
        scratch_shapes=[
            pltpu.VMEM((len(sides), length, full), BF16),
            pltpu.VMEM((lows, length, cols), F32),
        ],
        name="product",
    )(flips, lows_at, *sides, *blocks)


def reverse_bits(value, count):
    result = 0
    while count > 1:
        result, value, count = result * 2 + value % 2, value // 2, count // 2
    return result


def cycle_of(highs, lows):
    walk = [(high, 0) for high in range(highs)]
    for at in range(highs - 1, -1, -1):
        lows_at = range(1, lows) if (highs - 1 - at) % 2 == 0 else range(lows - 1, 0, -1)
        walk += [(at, low) for low in lows_at]
    return [high * lows + low for high, low in walk]


def body(
    tokens,
    embedding,
    norm_gain,
    in_weight,
    short_taps,
    decay_rates,
    residue,
    skip_weight,
    out_weight,
):
    ctx_count = lax.axis_size("ctx")
    fsdp_count = lax.axis_size("fsdp")
    lows = ctx_count // fsdp_count
    ctx_at = lax.axis_index("ctx")
    fsdp_at = lax.axis_index("fsdp")
    high_at, low_at = ctx_at // lows, ctx_at % lows
    tok_count = tokens.shape[0]
    _, columns = embedding.shape
    local_channels = in_weight.shape[2]
    part = local_channels // lows
    own = local_channels // ctx_count

    def move(value, target):
        return send(value, ctx_count, fsdp_count, target)

    by_kind = jnp.swapaxes(in_weight, 0, 1)
    weights = [lax.dynamic_slice_in_dim(by_kind, low_at * part, part, 2)]
    ids = [tokens[None, :]]
    for shift in range(1, lows):
        def neighbour(i, j):
            return (i // lows * lows + (i % lows - shift) % lows, j)

        going = lax.dynamic_slice_in_dim(by_kind, (low_at - shift) % lows * part, part, 2)
        weights.append(move(going, neighbour))
        ids.append(move(tokens[None, :], neighbour))

    chips = fsdp_count // 2
    across = None
    for shift in range(1, chips):
        got = move(
            embedding, lambda i, j: (i, (j + 2 * shift) % fsdp_count) if j == i // lows else None
        )
        across = got if across is None else across + got
    channel_at = low_at * part + high_at * own
    per_group = min(GROUP, own)
    group_count = own // per_group
    decay = lax.dynamic_slice_in_dim(decay_rates.T, channel_at // GROUP, group_count, 0)
    weight = lax.dynamic_slice_in_dim(residue.T, channel_at // GROUP, group_count, 0)
    filters = make_filters(decay, weight)
    taps = lax.dynamic_slice_in_dim(short_taps, channel_at, own, 2)
    taps = taps.reshape(taps.shape[0], 3 * own).T
    skip = lax.dynamic_slice_in_dim(skip_weight, channel_at, own, 0)[:, None]
    (across,) = after((across,), taps, skip, *filters)
    holder = jnp.where(fsdp_at == high_at, embedding, across)
    beside = move(holder, lambda i, j: (i, j ^ 1) if j % 2 == i // lows % 2 else None)
    gain = lax.dynamic_slice_in_dim(norm_gain, high_at * columns, columns, 0)[None, :]

    cycle = cycle_of(fsdp_count, lows)
    spot = {ctx: at for at, ctx in enumerate(cycle)}
    moved = move(
        out_weight,
        lambda i, j: ((reverse_bits(j, fsdp_count) ^ i // lows) * lows + i % lows, i // lows),
    )
    ahead, behind = [moved], [moved]
    rounds = (ctx_count - 1) // 2

    def turn(*others):
        low, high = after((ahead[-1], behind[-1]), *others)
        ahead.append(move(low, lambda i, j: (cycle[(spot[i] + 1) % ctx_count], j)))
        behind.append(move(high, lambda i, j: (cycle[(spot[i] - 1) % ctx_count], j)))

    turn()
    origin = jnp.where(fsdp_at == high_at, 0, jnp.where((fsdp_at - high_at) % 2 == 0, 1, 2))
    partial = make_table(
        jnp.stack([low_at, origin]), embedding, across, beside, gain, weights, ids, fsdp_count
    )
    pieces = [lax.dynamic_index_in_dim(partial, high_at, 0, keepdims=False)]
    for shift in range(1, fsdp_count):
        going = lax.dynamic_index_in_dim(partial, (high_at + shift) % fsdp_count, 0, keepdims=False)
        pieces.append(move(going, lambda i, j: ((i // lows + shift) % fsdp_count * lows + i % lows, j)))

    for _ in range(1, rounds - 1):
        pieces = list(after(pieces, ahead[-1], behind[-1]))
        turn(*pieces)
    ctx_place = jnp.stack([ctx_at, jnp.int32(lows)])
    gated = make_mixer(
        ctx_place, columns * fsdp_count, tok_count, taps, skip, filters, pieces, ctx_count
    )

    pieces = [lax.dynamic_slice_in_dim(gated, ctx_at * tok_count, tok_count, 1)]
    for shift in range(1, ctx_count):
        going = lax.dynamic_slice_in_dim(gated, (ctx_at + shift) % ctx_count * tok_count, tok_count, 1)
        pieces.append(move(going, lambda i, j: ((i + shift) % ctx_count, j)))
    turn(pieces[-1])
    middle = out_weight.shape[0] // 2
    last_ahead = move(ahead[-1][:middle], lambda i, j: (cycle[(spot[i] + 1) % ctx_count], j))
    last_behind = move(behind[-1][middle:], lambda i, j: (cycle[(spot[i] - 1) % ctx_count], j))
    blocks = ahead + behind[1:] + [last_ahead, last_behind]
    steps = list(range(len(ahead))) + [-at for at in range(1, len(behind))] + [len(ahead)] * 2
    from_ctx = [[cycle[(spot[ctx] - step) % ctx_count] for step in steps] for ctx in range(ctx_count)]
    sources = jnp.array(from_ctx, jnp.int32)[ctx_at]
    lows_from = sources % lows
    to_flip = [
        [reverse_bits(high ^ j, fsdp_count) ^ j for high in range(fsdp_count)] for j in range(fsdp_count)
    ]
    flips = jnp.array(to_flip, jnp.int32)[fsdp_at][sources // lows]

    ordered = make_order(ctx_place, pieces)
    sides, order = [ordered], [0]
    reach = fsdp_count // 2
    while reach:
        sides = sides + [move(side, lambda i, j: (i, j ^ reach)) for side in sides]
        order = order + [at ^ reach for at in order]
        reach //= 2
    return make_product(flips, lows_from, tuple(order), sides, blocks, lows)


def solution(mesh):
    placed = (
        P("ctx"),
        P(None, "fsdp"),
        P(),
        P("ctx", None, "fsdp"),
        P(None, None, "fsdp"),
        P(None, "fsdp"),
        P(None, "fsdp"),
        P("fsdp"),
        P("fsdp", "ctx"),
    )
    return jax.shard_map(body, mesh=mesh, in_specs=placed, out_specs=P("ctx", "fsdp"), check_vma=False)
```

```python
import functools

import jax
import jax.numpy as jnp
from jax import lax
from jax.experimental import pallas as pl
from jax.experimental.pallas import tpu as pltpu
from jax.sharding import PartitionSpec as P


GROUP = 16
CHUNK = 256
TILE = 512
EXTRA = 16
PLACES = 4
BASE = 16
AXES = ("ctx", "fsdp")
BF16 = jnp.bfloat16
F32 = jnp.float32


def send(value, ctx_count, fsdp_count, target):
    pairs = []
    for i in range(ctx_count):
        for j in range(fsdp_count):
            to = target(i, j)
            if to is not None:
                pairs.append((i * fsdp_count + j, to[0] * fsdp_count + to[1]))
    return lax.ppermute(value, AXES, pairs)


def after(values, *others):
    return lax.optimization_barrier((tuple(values), others))[0]


def split_high_low(value):
    high = value.astype(BF16)
    return high, (value - high.astype(F32)).astype(BF16)


def filter_body(
    decay_ref, residue_ref, decay_col_ref, residue_col_ref, taps_ref, skip_ref,
    near_ref, into_ref, outof_ref, step_ref, side_ref,
):
    count = taps_ref.shape[1]
    side_ref[:, :count] = taps_ref[...]
    side_ref[:skip_ref.shape[0], count:count + 1] = skip_ref[...]
    groups, modes = decay_ref.shape
    rows = lax.broadcasted_iota(jnp.int32, (CHUNK, CHUNK), 0)
    cols = lax.broadcasted_iota(jnp.int32, (CHUNK, CHUNK), 1)
    lag = (cols - rows).astype(F32)
    clipped = jnp.maximum(lag, 0.0)
    back = (CHUNK - 1 - lax.broadcasted_iota(jnp.int32, (CHUNK, modes), 0)).astype(F32)
    ahead = (1 + lax.broadcasted_iota(jnp.int32, (modes, CHUNK), 1)).astype(F32)
    for group in range(groups):
        total = jnp.zeros((CHUNK, CHUNK), F32)
        for mode in range(modes):
            total += residue_ref[group, mode] * jnp.exp(-decay_ref[group, mode] * clipped)
        near_ref[group] = jnp.where(lag >= 0.0, total, 0.0).astype(BF16)
        rate_row = decay_col_ref[group, 0:1, :]
        into_high, into_low = split_high_low(jnp.exp(-rate_row * back))
        into_ref[group] = jnp.concatenate([into_high, into_low], axis=1)
        rate_col = jnp.swapaxes(jnp.broadcast_to(rate_row, (8, modes)), 0, 1)[:, 0:1]
        residue_row = residue_col_ref[group, 0:1, :]
        residue_col = jnp.swapaxes(jnp.broadcast_to(residue_row, (8, modes)), 0, 1)[:, 0:1]
        outof_high, outof_low = split_high_low(residue_col * jnp.exp(-rate_col * ahead))
        outof_ref[group] = jnp.concatenate([outof_high, outof_high, outof_low], axis=0)
        step_ref[group] = jnp.exp(-rate_row * CHUNK)


def make_filters(decay, residue, taps, skip):
    groups, modes = decay.shape
    smem = pl.BlockSpec(memory_space=pltpu.SMEM)
    vmem = pl.BlockSpec(memory_space=pltpu.VMEM)
    return pl.pallas_call(
        filter_body,
        in_specs=[smem, smem] + [vmem] * 4,
        out_specs=[vmem] * 5,
        out_shape=[
            jax.ShapeDtypeStruct((groups, CHUNK, CHUNK), BF16),
            jax.ShapeDtypeStruct((groups, CHUNK, 2 * modes), BF16),
            jax.ShapeDtypeStruct((groups, 3 * modes, CHUNK), BF16),
            jax.ShapeDtypeStruct((groups, 1, modes), F32),
            jax.ShapeDtypeStruct((taps.shape[0], 128), F32),
        ],
        name="filters",
    )(decay, residue, decay[:, None, :], residue[:, None, :], taps, skip)


def table_body(count, place_ref, own_ref, across_ref, beside_ref, gain_ref, *refs):
    raw_ref, scaled_ref, extra_ref, flip_ref = refs[-4:]
    weight_refs, token_refs, out_refs = refs[:count], refs[count:2 * count], refs[2 * count:-4]
    vocab, columns = own_ref.shape
    width = columns // count
    pieces, rows = len(out_refs), out_refs[0].shape[0]
    low_at, origin, high_at = place_ref[0], place_ref[1], place_ref[3]

    @pl.when(origin == 0)
    def _():
        raw_ref[...] = own_ref[...].astype(F32)

    @pl.when(origin == 1)
    def _():
        raw_ref[...] = across_ref[...].astype(F32)

    @pl.when(origin == 2)
    def _():
        raw_ref[...] = beside_ref[...].astype(F32)

    raw = raw_ref[...]
    scaled_ref[...] = (raw * gain_ref[...]).astype(BF16)
    extra_ref[...] = jnp.zeros_like(extra_ref)
    squares = jnp.broadcast_to(jnp.sum(raw * raw, axis=1, keepdims=True), (vocab, 128))
    squares = jnp.swapaxes(squares, 0, 1)[0:1, :]
    for row in range(3):
        rounded = squares.astype(BF16).astype(F32)
        extra_ref[row:row + 1, :] = rounded
        squares = squares - rounded
    for shift, token_ref in enumerate(token_refs):
        low = lax.rem(low_at + shift, count)
        extra_ref[pl.ds(3 + low, 1), :] = (token_ref[...] // BASE).astype(F32)
        extra_ref[pl.ds(3 + count + low, 1), :] = (token_ref[...] % BASE).astype(F32)
    extra = extra_ref[...].astype(BF16)
    each = (rows - EXTRA) // 3
    for out_ref in out_refs:
        out_ref[:EXTRA, :] = extra
    for kind in range(3):
        total = None
        for shift, weight_ref in enumerate(weight_refs):
            start = pl.multiple_of(lax.rem(low_at + shift, count) * width, width)
            part = jnp.dot(scaled_ref[:, pl.ds(start, width)], weight_ref[kind], preferred_element_type=F32)
            total = part if total is None else total + part
        flip_ref[...] = jnp.swapaxes(total, 0, 1)
        for shift, out_ref in enumerate(out_refs):
            start = pl.multiple_of(lax.rem(high_at + shift, pieces) * each, each)
            out_ref[EXTRA + kind * each:EXTRA + (kind + 1) * each, :] = flip_ref[pl.ds(start, each), :].astype(BF16)


def make_table(place, own, across, beside, gain, weights, tokens, pieces):
    vocab = own.shape[0]
    channels = weights[0].shape[2]
    vmem = pl.BlockSpec(memory_space=pltpu.VMEM)
    return pl.pallas_call(
        functools.partial(table_body, len(weights)),
        in_specs=[pl.BlockSpec(memory_space=pltpu.SMEM)] + [vmem] * (4 + len(weights) + len(tokens)),
        out_specs=[vmem] * pieces,
        out_shape=[jax.ShapeDtypeStruct((EXTRA + 3 * channels // pieces, vocab), BF16)] * pieces,
        scratch_shapes=[
            pltpu.VMEM(own.shape, F32),
            pltpu.VMEM(own.shape, BF16),
            pltpu.VMEM((EXTRA, vocab), F32),
            pltpu.VMEM((channels, vocab), F32),
        ],
        name="table",
    )(place, own, across, beside, gain, *weights, *tokens)


def mixer_body(width, taps, place_ref, near_ref, into_ref, outof_ref, step_ref, taps_ref, *refs):
    query_ref, drive_ref, conv_ref, token_ref, stage_ref = refs[-5:]
    ctx_at = place_ref[2]
    out_refs = refs[-5 - token_ref.shape[0]:-5]
    piece_refs = refs[:-5 - token_ref.shape[0]]
    rows, vocab = piece_refs[0].shape
    rows -= EXTRA
    channels = rows // 3
    blocks, _, block = token_ref.shape
    length = blocks * block
    count = len(piece_refs)
    lows = blocks // count
    total = None
    squares = None
    for shift, ref in enumerate(piece_refs):
        head = ref[:EXTRA, :].astype(F32)
        summed = head[0:1] + head[1:2] + head[2:3]
        squares = summed if squares is None else squares + summed
        high = lax.rem(ctx_at // lows - shift + count, count)
        for low in range(lows):
            ids = head[3 + low:4 + low] * BASE + head[3 + lows + low:4 + lows + low]
            token_ref[high * lows + low] = ids[:, :block].astype(jnp.int32)
        part = ref[EXTRA:, :].astype(F32)
        total = part if total is None else total + part
    table = (total * lax.rsqrt(squares * (1.0 / width) + 1e-05)).astype(BF16)
    ids = lax.broadcasted_iota(jnp.int32, (vocab, TILE), 0)
    halo = jnp.zeros((rows, 128), F32)
    for tile in range(length // TILE):
        at = tile * TILE
        inside = at % block
        tokens = token_ref[at // block][:, inside:inside + TILE]
        hot = jnp.where(ids == tokens, 1.0, 0.0).astype(BF16)
        projected = jnp.dot(table, hot, preferred_element_type=F32)
        extended = jnp.concatenate([halo, projected], axis=1)
        halo = projected[:, TILE - 128:]
        short = taps_ref[:, 0:1] * projected
        for lag in range(1, taps):
            short += taps_ref[:, lag:lag + 1] * pltpu.roll(extended, lag, 1)[:, 128:]
        query_ref[:, at:at + TILE] = short[:channels]
        drive_ref[:, at:at + TILE] = short[channels:2 * channels] * short[2 * channels:]
    groups = near_ref.shape[0]
    per = channels // groups
    modes = step_ref.shape[2]
    chunks = length // CHUNK
    for group in range(groups):
        base = group * per
        stacked = jnp.concatenate(
            [drive_ref[base:base + per, n * CHUNK:(n + 1) * CHUNK] for n in range(chunks)], axis=0
        ).astype(BF16)
        both = jnp.dot(stacked, into_ref[group], preferred_element_type=F32)
        ends = both[:, :modes] + both[:, modes:]
        step = step_ref[group]
        state = jnp.zeros((per, modes), F32)
        starts = []
        for n in range(chunks):
            starts.append(state)
            state = state * step + ends[n * per:(n + 1) * per]
        high, low = split_high_low(jnp.concatenate(starts, axis=0))
        conv_ref[...] = jnp.dot(stacked, near_ref[group], preferred_element_type=F32) + jnp.dot(
            jnp.concatenate([high, low, high], axis=1), outof_ref[group], preferred_element_type=F32
        )
        for n in range(chunks):
            here = slice(n * CHUNK, (n + 1) * CHUNK)
            response = conv_ref[n * per:(n + 1) * per, :] + taps_ref[base:base + per, taps:taps + 1] * drive_ref[base:base + per, here]
            at = n * CHUNK
            stage_ref[at // block, base:base + per, at % block:at % block + CHUNK] = (
                query_ref[base:base + per, here] * response
            ).astype(BF16)
    for shift, out_ref in enumerate(out_refs):
        out_ref[...] = stage_ref[lax.rem(ctx_at + shift, blocks)]


def make_mixer(place, width, taps, block, filters, pieces, blocks):
    rows = pieces[0].shape[0] - EXTRA
    channels = rows // 3
    length = block * blocks
    groups = filters[0].shape[0]
    vmem = pl.BlockSpec(memory_space=pltpu.VMEM)
    return pl.pallas_call(
        functools.partial(mixer_body, width, taps),
        in_specs=[pl.BlockSpec(memory_space=pltpu.SMEM)] + [vmem] * (5 + len(pieces)),
        out_specs=[vmem] * blocks,
        out_shape=[jax.ShapeDtypeStruct((channels, block), BF16)] * blocks,
        scratch_shapes=[
            pltpu.VMEM((channels, length), F32),
            pltpu.VMEM((channels, length), F32),
            pltpu.VMEM((length // CHUNK * (channels // groups), CHUNK), F32),
            pltpu.VMEM((blocks, 1, block), jnp.int32),
            pltpu.VMEM((blocks, channels, block), BF16),
        ],
        name="mixer",
    )(place, *filters, *pieces)


def order_body(lows, place_ref, *refs):
    piece_refs, out_ref, stage_ref = refs[:-2], refs[-2], refs[-1]
    count = len(piece_refs)
    rows = piece_refs[0].shape[0]
    for shift, ref in enumerate(piece_refs):
        source = lax.rem(place_ref[2] - shift + count, count)
        start = pl.multiple_of((lax.rem(source, lows) * (count // lows) + source // lows) * rows, rows)
        stage_ref[pl.ds(start, rows), :] = ref[...].astype(F32)
    out_ref[...] = jnp.swapaxes(stage_ref[...], 0, 1).astype(BF16)


def make_order(place, pieces, lows):
    rows, length = pieces[0].shape
    vmem = pl.BlockSpec(memory_space=pltpu.VMEM)
    return pl.pallas_call(
        functools.partial(order_body, lows),
        in_specs=[pl.BlockSpec(memory_space=pltpu.SMEM)] + [vmem] * len(pieces),
        out_specs=vmem,
        out_shape=jax.ShapeDtypeStruct((length, rows * len(pieces)), BF16),
        scratch_shapes=[pltpu.VMEM((rows * len(pieces), length), F32)],
        name="order",
    )(place, *pieces)


def product_body(order, place_ref, *refs):
    side_refs = refs[:len(order)]
    block_refs = refs[len(order):-3]
    out_ref, sides_ref, sum_ref = refs[-3:]
    for flip, ref in zip(order, side_refs):
        sides_ref[flip] = ref[...]
    full, cols = block_refs[0].shape
    sum_ref[...] = jnp.zeros_like(sum_ref)
    for at, ref in enumerate(block_refs):
        first = full // 2 if at == len(block_refs) - 1 else 0
        side = sides_ref[place_ref[PLACES + at], :, first:first + ref.shape[0]]
        sum_ref[place_ref[PLACES + len(block_refs) + at]] += jnp.dot(side, ref[...], preferred_element_type=F32)
    for low in range(sum_ref.shape[0]):
        out_ref[:, low * cols:(low + 1) * cols] = sum_ref[low].astype(BF16)


def make_product(place, order, sides, blocks, lows):
    length, full = sides[0].shape
    cols = blocks[0].shape[1]
    smem = pl.BlockSpec(memory_space=pltpu.SMEM)
    vmem = pl.BlockSpec(memory_space=pltpu.VMEM)
    return pl.pallas_call(
        functools.partial(product_body, order),
        in_specs=[smem] + [vmem] * (len(sides) + len(blocks)),
        out_specs=vmem,
        out_shape=jax.ShapeDtypeStruct((length, lows * cols), BF16),
        scratch_shapes=[
            pltpu.VMEM((len(sides), length, full), BF16),
            pltpu.VMEM((lows, length, cols), F32),
        ],
        name="product",
    )(place, *sides, *blocks)


def reverse_bits(value, count):
    result = 0
    while count > 1:
        result, value, count = result * 2 + value % 2, value // 2, count // 2
    return result


def cycle_of(highs, lows):
    walk = [(high, 0) for high in range(highs)]
    for at in range(highs - 1, -1, -1):
        lows_at = range(1, lows) if (highs - 1 - at) % 2 == 0 else range(lows - 1, 0, -1)
        walk += [(at, low) for low in lows_at]
    return [high * lows + low for high, low in walk]


def body(
    tokens,
    embedding,
    norm_gain,
    in_weight,
    short_taps,
    decay_rates,
    residue,
    skip_weight,
    out_weight,
):
    ctx_count = lax.axis_size("ctx")
    fsdp_count = lax.axis_size("fsdp")
    lows = ctx_count // fsdp_count
    ctx_at = lax.axis_index("ctx")
    fsdp_at = lax.axis_index("fsdp")
    high_at, low_at = ctx_at // lows, ctx_at % lows
    tok_count = tokens.shape[0]
    _, columns = embedding.shape
    local_channels = in_weight.shape[2]
    part = local_channels // lows
    own = local_channels // ctx_count

    def move(value, target):
        return send(value, ctx_count, fsdp_count, target)

    by_kind = jnp.swapaxes(in_weight, 0, 1)
    weights = [lax.dynamic_slice_in_dim(by_kind, low_at * part, part, 2)]
    ids = [tokens[None, :]]
    for shift in range(1, lows):
        def neighbour(i, j):
            return (i // lows * lows + (i % lows - shift) % lows, j)

        going = lax.dynamic_slice_in_dim(by_kind, (low_at - shift) % lows * part, part, 2)
        weights.append(move(going, neighbour))
        ids.append(move(tokens[None, :], neighbour))

    chips = fsdp_count // 2
    across = None
    for shift in range(1, chips):
        got = move(
            embedding, lambda i, j: (i, (j + 2 * shift) % fsdp_count) if j == i // lows else None
        )
        across = got if across is None else across + got
    cycle = cycle_of(fsdp_count, lows)
    spot = {ctx: at for at, ctx in enumerate(cycle)}
    moved = move(
        out_weight,
        lambda i, j: ((reverse_bits(j, fsdp_count) ^ i // lows) * lows + i % lows, i // lows),
    )
    ahead, behind = [moved], [moved]
    rounds = (ctx_count - 1) // 2
    steps = [*range(rounds + 1), *range(-1, -rounds - 1, -1), rounds + 1, rounds + 1]
    known = []
    for i in range(ctx_count):
        met = [cycle[(spot[i] - step) % ctx_count] for step in steps]
        for j in range(fsdp_count):
            origin = 0 if j == i // lows else 1 if (j - i // lows) % 2 == 0 else 2
            flips = [reverse_bits(ctx // lows ^ j, fsdp_count) ^ j for ctx in met]
            known.append([i % lows, origin, i, i // lows, *flips, *(ctx % lows for ctx in met)])
    place = jnp.array(known, jnp.int32)[ctx_at * fsdp_count + fsdp_at]

    channel_at = low_at * part + high_at * own
    per_group = min(GROUP, own)
    group_count = own // per_group
    decay = lax.dynamic_slice_in_dim(decay_rates.T, channel_at // GROUP, group_count, 0)
    weight = lax.dynamic_slice_in_dim(residue.T, channel_at // GROUP, group_count, 0)
    taps = lax.dynamic_slice_in_dim(short_taps, channel_at, own, 2)
    taps = taps.reshape(taps.shape[0], 3 * own).T
    skip = lax.dynamic_slice_in_dim(skip_weight, channel_at, own, 0)[:, None]
    gain = lax.dynamic_slice_in_dim(norm_gain, high_at * columns, columns, 0)[None, :]
    filters = make_filters(decay, weight, taps, skip)
    (across,) = after((across,), gain, place, *filters)
    holder = jnp.where(fsdp_at == high_at, embedding, across)
    beside = move(holder, lambda i, j: (i, j ^ 1) if j % 2 == i // lows % 2 else None)

    def turn(*others):
        low, high = after((ahead[-1], behind[-1]), *others)
        ahead.append(move(low, lambda i, j: (cycle[(spot[i] + 1) % ctx_count], j)))
        behind.append(move(high, lambda i, j: (cycle[(spot[i] - 1) % ctx_count], j)))

    turn()
    outgoing = make_table(place, embedding, across, beside, gain, weights, ids, fsdp_count)
    pieces = [outgoing[0]]
    for shift in range(1, fsdp_count):
        pieces.append(
            move(outgoing[shift], lambda i, j: ((i // lows + shift) % fsdp_count * lows + i % lows, j))
        )

    for _ in range(1, rounds - 1):
        pieces = list(after(pieces, ahead[-1], behind[-1]))
        turn(*pieces)
    gated = make_mixer(
        place, columns * fsdp_count, short_taps.shape[0], tok_count, filters, pieces, ctx_count
    )

    pieces = [gated[0]]
    for shift in range(1, ctx_count):
        pieces.append(move(gated[shift], lambda i, j: ((i + shift) % ctx_count, j)))
    pieces = list(after(pieces, ahead[-1], behind[-1]))
    turn(gated[0])
    ordered = make_order(place, pieces, lows)
    middle = out_weight.shape[0] // 2
    low, high = after((ahead[-1], behind[-1]), ordered)
    last_ahead = move(low[:middle], lambda i, j: (cycle[(spot[i] + 1) % ctx_count], j))
    last_behind = move(high[middle:], lambda i, j: (cycle[(spot[i] - 1) % ctx_count], j))
    blocks = ahead + behind[1:] + [last_ahead, last_behind]
    sides, order = [ordered], [0]
    reach = fsdp_count // 2
    while reach:
        more = []
        for side in sides:
            more.append(move(side, lambda i, j: (i, j ^ reach)))
        sides = sides + more
        order = order + [at ^ reach for at in order]
        reach //= 2
    return make_product(place, tuple(order), sides, blocks, lows)


def solution(mesh):
    placed = (
        P("ctx"),
        P(None, "fsdp"),
        P(),
        P("ctx", None, "fsdp"),
        P(None, None, "fsdp"),
        P(None, "fsdp"),
        P(None, "fsdp"),
        P("fsdp"),
        P("fsdp", "ctx"),
    )
    return jax.shard_map(body, mesh=mesh, in_specs=placed, out_specs=P("ctx", "fsdp"), check_vma=False)
```

```python
import functools

import jax
import jax.numpy as jnp
from jax import lax
from jax.experimental import pallas as pl
from jax.experimental.pallas import tpu as pltpu
from jax.sharding import PartitionSpec as P


GROUP = 16
CHUNK = 256
TILE = 512
EXTRA = 16
PLACES = 4
BASE = 16
AXES = ("ctx", "fsdp")
BF16 = jnp.bfloat16
F32 = jnp.float32


def send(value, ctx_count, fsdp_count, target):
    pairs = []
    for i in range(ctx_count):
        for j in range(fsdp_count):
            to = target(i, j)
            if to is not None:
                pairs.append((i * fsdp_count + j, to[0] * fsdp_count + to[1]))
    return lax.ppermute(value, AXES, pairs)


def after(values, *others):
    return lax.optimization_barrier((tuple(values), others))[0]


def near(*values):
    return [pltpu.with_memory_space_constraint(value, pltpu.VMEM) for value in values]


def split_high_low(value):
    high = value.astype(BF16)
    return high, (value - high.astype(F32)).astype(BF16)


def filter_body(
    decay_ref, residue_ref, decay_col_ref, residue_col_ref, taps_ref, skip_ref,
    near_ref, into_ref, outof_ref, step_ref, side_ref,
):
    count = taps_ref.shape[1]
    side_ref[:, :count] = taps_ref[...]
    side_ref[:skip_ref.shape[0], count:count + 1] = skip_ref[...]
    groups, modes = decay_ref.shape
    rows = lax.broadcasted_iota(jnp.int32, (CHUNK, CHUNK), 0)
    cols = lax.broadcasted_iota(jnp.int32, (CHUNK, CHUNK), 1)
    lag = (cols - rows).astype(F32)
    clipped = jnp.maximum(lag, 0.0)
    back = (CHUNK - 1 - lax.broadcasted_iota(jnp.int32, (CHUNK, modes), 0)).astype(F32)
    ahead = (1 + lax.broadcasted_iota(jnp.int32, (modes, CHUNK), 1)).astype(F32)
    for group in range(groups):
        total = jnp.zeros((CHUNK, CHUNK), F32)
        for mode in range(modes):
            total += residue_ref[group, mode] * jnp.exp(-decay_ref[group, mode] * clipped)
        near_ref[group] = jnp.where(lag >= 0.0, total, 0.0).astype(BF16)
        rate_row = decay_col_ref[group, 0:1, :]
        into_high, into_low = split_high_low(jnp.exp(-rate_row * back))
        into_ref[group] = jnp.concatenate([into_high, into_low], axis=1)
        rate_col = jnp.swapaxes(jnp.broadcast_to(rate_row, (8, modes)), 0, 1)[:, 0:1]
        residue_row = residue_col_ref[group, 0:1, :]
        residue_col = jnp.swapaxes(jnp.broadcast_to(residue_row, (8, modes)), 0, 1)[:, 0:1]
        outof_high, outof_low = split_high_low(residue_col * jnp.exp(-rate_col * ahead))
        outof_ref[group] = jnp.concatenate([outof_high, outof_high, outof_low], axis=0)
        step_ref[group] = jnp.exp(-rate_row * CHUNK)


def make_filters(decay, residue, taps, skip):
    groups, modes = decay.shape
    smem = pl.BlockSpec(memory_space=pltpu.SMEM)
    vmem = pl.BlockSpec(memory_space=pltpu.VMEM)
    return pl.pallas_call(
        filter_body,
        in_specs=[smem, smem] + [vmem] * 4,
        out_specs=[vmem] * 5,
        out_shape=[
            jax.ShapeDtypeStruct((groups, CHUNK, CHUNK), BF16),
            jax.ShapeDtypeStruct((groups, CHUNK, 2 * modes), BF16),
            jax.ShapeDtypeStruct((groups, 3 * modes, CHUNK), BF16),
            jax.ShapeDtypeStruct((groups, 1, modes), F32),
            jax.ShapeDtypeStruct((taps.shape[0], 128), F32),
        ],
        name="filters",
    )(decay, residue, decay[:, None, :], residue[:, None, :], taps, skip)


def table_body(count, place_ref, own_ref, across_ref, beside_ref, gain_ref, *refs):
    raw_ref, scaled_ref, extra_ref, flip_ref = refs[-4:]
    weight_refs, token_refs, out_refs = refs[:count], refs[count:2 * count], refs[2 * count:-4]
    vocab, columns = own_ref.shape
    width = columns // count
    pieces, rows = len(out_refs), out_refs[0].shape[0]
    low_at, origin, high_at = place_ref[0], place_ref[1], place_ref[3]

    @pl.when(origin == 0)
    def _():
        raw_ref[...] = own_ref[...].astype(F32)

    @pl.when(origin == 1)
    def _():
        raw_ref[...] = across_ref[...].astype(F32)

    @pl.when(origin == 2)
    def _():
        raw_ref[...] = beside_ref[...].astype(F32)

    raw = raw_ref[...]
    scaled_ref[...] = (raw * gain_ref[...]).astype(BF16)
    extra_ref[...] = jnp.zeros_like(extra_ref)
    squares = jnp.broadcast_to(jnp.sum(raw * raw, axis=1, keepdims=True), (vocab, 128))
    squares = jnp.swapaxes(squares, 0, 1)[0:1, :]
    for row in range(3):
        rounded = squares.astype(BF16).astype(F32)
        extra_ref[row:row + 1, :] = rounded
        squares = squares - rounded
    for shift, token_ref in enumerate(token_refs):
        low = lax.rem(low_at + shift, count)
        extra_ref[pl.ds(3 + low, 1), :] = (token_ref[...] // BASE).astype(F32)
        extra_ref[pl.ds(3 + count + low, 1), :] = (token_ref[...] % BASE).astype(F32)
    extra = extra_ref[...].astype(BF16)
    each = (rows - EXTRA) // 3
    for out_ref in out_refs:
        out_ref[:EXTRA, :] = extra
    for kind in range(3):
        total = None
        for shift, weight_ref in enumerate(weight_refs):
            start = pl.multiple_of(lax.rem(low_at + shift, count) * width, width)
            part = jnp.dot(scaled_ref[:, pl.ds(start, width)], weight_ref[kind], preferred_element_type=F32)
            total = part if total is None else total + part
        flip_ref[...] = jnp.swapaxes(total, 0, 1)
        for shift, out_ref in enumerate(out_refs):
            start = pl.multiple_of(lax.rem(high_at + shift, pieces) * each, each)
            out_ref[EXTRA + kind * each:EXTRA + (kind + 1) * each, :] = flip_ref[pl.ds(start, each), :].astype(BF16)


def make_table(place, own, across, beside, gain, weights, tokens, pieces):
    vocab = own.shape[0]
    channels = weights[0].shape[2]
    vmem = pl.BlockSpec(memory_space=pltpu.VMEM)
    return pl.pallas_call(
        functools.partial(table_body, len(weights)),
        in_specs=[pl.BlockSpec(memory_space=pltpu.SMEM)] + [vmem] * (4 + len(weights) + len(tokens)),
        out_specs=[vmem] * pieces,
        out_shape=[pltpu.VMEM((EXTRA + 3 * channels // pieces, vocab), BF16)] * pieces,
        scratch_shapes=[
            pltpu.VMEM(own.shape, F32),
            pltpu.VMEM(own.shape, BF16),
            pltpu.VMEM((EXTRA, vocab), F32),
            pltpu.VMEM((channels, vocab), F32),
        ],
        name="table",
    )(place, own, across, beside, gain, *weights, *tokens)


def mixer_body(width, taps, place_ref, near_ref, into_ref, outof_ref, step_ref, taps_ref, *refs):
    query_ref, drive_ref, conv_ref, token_ref, stage_ref = refs[-5:]
    ctx_at = place_ref[2]
    out_refs = refs[-5 - token_ref.shape[0]:-5]
    piece_refs = refs[:-5 - token_ref.shape[0]]
    rows, vocab = piece_refs[0].shape
    rows -= EXTRA
    channels = rows // 3
    blocks, _, block = token_ref.shape
    length = blocks * block
    count = len(piece_refs)
    lows = blocks // count
    total = None
    squares = None
    for shift, ref in enumerate(piece_refs):
        head = ref[:EXTRA, :].astype(F32)
        summed = head[0:1] + head[1:2] + head[2:3]
        squares = summed if squares is None else squares + summed
        high = lax.rem(ctx_at // lows - shift + count, count)
        for low in range(lows):
            ids = head[3 + low:4 + low] * BASE + head[3 + lows + low:4 + lows + low]
            token_ref[high * lows + low] = ids[:, :block].astype(jnp.int32)
        part = ref[EXTRA:, :].astype(F32)
        total = part if total is None else total + part
    table = (total * lax.rsqrt(squares * (1.0 / width) + 1e-05)).astype(BF16)
    ids = lax.broadcasted_iota(jnp.int32, (vocab, TILE), 0)
    halo = jnp.zeros((rows, 128), F32)
    for tile in range(length // TILE):
        at = tile * TILE
        inside = at % block
        tokens = token_ref[at // block][:, inside:inside + TILE]
        hot = jnp.where(ids == tokens, 1.0, 0.0).astype(BF16)
        projected = jnp.dot(table, hot, preferred_element_type=F32)
        extended = jnp.concatenate([halo, projected], axis=1)
        halo = projected[:, TILE - 128:]
        short = taps_ref[:, 0:1] * projected
        for lag in range(1, taps):
            short += taps_ref[:, lag:lag + 1] * pltpu.roll(extended, lag, 1)[:, 128:]
        query_ref[:, at:at + TILE] = short[:channels]
        drive_ref[:, at:at + TILE] = short[channels:2 * channels] * short[2 * channels:]
    groups = near_ref.shape[0]
    per = channels // groups
    modes = step_ref.shape[2]
    chunks = length // CHUNK
    for group in range(groups):
        base = group * per
        stacked = jnp.concatenate(
            [drive_ref[base:base + per, n * CHUNK:(n + 1) * CHUNK] for n in range(chunks)], axis=0
        ).astype(BF16)
        both = jnp.dot(stacked, into_ref[group], preferred_element_type=F32)
        ends = both[:, :modes] + both[:, modes:]
        step = step_ref[group]
        state = jnp.zeros((per, modes), F32)
        starts = []
        for n in range(chunks):
            starts.append(state)
            state = state * step + ends[n * per:(n + 1) * per]
        high, low = split_high_low(jnp.concatenate(starts, axis=0))
        conv_ref[...] = jnp.dot(stacked, near_ref[group], preferred_element_type=F32) + jnp.dot(
            jnp.concatenate([high, low, high], axis=1), outof_ref[group], preferred_element_type=F32
        )
        for n in range(chunks):
            here = slice(n * CHUNK, (n + 1) * CHUNK)
            response = conv_ref[n * per:(n + 1) * per, :] + taps_ref[base:base + per, taps:taps + 1] * drive_ref[base:base + per, here]
            at = n * CHUNK
            stage_ref[at // block, base:base + per, at % block:at % block + CHUNK] = (
                query_ref[base:base + per, here] * response
            ).astype(BF16)
    for shift, out_ref in enumerate(out_refs):
        out_ref[...] = stage_ref[lax.rem(ctx_at + shift, blocks)]


def make_mixer(place, width, taps, block, filters, pieces, blocks):
    rows = pieces[0].shape[0] - EXTRA
    channels = rows // 3
    length = block * blocks
    groups = filters[0].shape[0]
    vmem = pl.BlockSpec(memory_space=pltpu.VMEM)
    return pl.pallas_call(
        functools.partial(mixer_body, width, taps),
        in_specs=[pl.BlockSpec(memory_space=pltpu.SMEM)] + [vmem] * (5 + len(pieces)),
        out_specs=[vmem] * blocks,
        out_shape=[pltpu.VMEM((channels, block), BF16)] * blocks,
        scratch_shapes=[
            pltpu.VMEM((channels, length), F32),
            pltpu.VMEM((channels, length), F32),
            pltpu.VMEM((length // CHUNK * (channels // groups), CHUNK), F32),
            pltpu.VMEM((blocks, 1, block), jnp.int32),
            pltpu.VMEM((blocks, channels, block), BF16),
        ],
        name="mixer",
    )(place, *filters, *near(*pieces))


def order_body(lows, place_ref, *refs):
    piece_refs, out_ref, stage_ref = refs[:-2], refs[-2], refs[-1]
    count = len(piece_refs)
    rows = piece_refs[0].shape[0]
    for shift, ref in enumerate(piece_refs):
        source = lax.rem(place_ref[2] - shift + count, count)
        start = pl.multiple_of((lax.rem(source, lows) * (count // lows) + source // lows) * rows, rows)
        stage_ref[pl.ds(start, rows), :] = ref[...].astype(F32)
    out_ref[...] = jnp.swapaxes(stage_ref[...], 0, 1).astype(BF16)


def make_order(place, pieces, lows):
    rows, length = pieces[0].shape
    vmem = pl.BlockSpec(memory_space=pltpu.VMEM)
    return pl.pallas_call(
        functools.partial(order_body, lows),
        in_specs=[pl.BlockSpec(memory_space=pltpu.SMEM)] + [vmem] * len(pieces),
        out_specs=vmem,
        out_shape=pltpu.VMEM((length, rows * len(pieces)), BF16),
        scratch_shapes=[pltpu.VMEM((rows * len(pieces), length), F32)],
        name="order",
    )(place, *near(*pieces))


def product_body(order, place_ref, *refs):
    side_refs = refs[:len(order)]
    out_ref, sides_ref, sum_ref, wide_ref, arrived = refs[-5:]
    block_refs = refs[len(order):-5]
    full, cols = block_refs[0].shape
    copies = []
    for at, ref in enumerate(block_refs):
        copies.append(
            pltpu.make_async_copy(ref, wide_ref.at[at, :ref.shape[0]], arrived.at[at])
        )
        copies[-1].start()
    for flip, ref in zip(order, side_refs):
        sides_ref[flip] = ref[...]
    sum_ref[...] = jnp.zeros_like(sum_ref)
    for at, ref in enumerate(block_refs):
        rows = ref.shape[0]
        first = full // 2 if at == len(block_refs) - 1 else 0
        copies[at].wait()
        side = sides_ref[place_ref[PLACES + at], :, first:first + rows]
        sum_ref[place_ref[PLACES + len(block_refs) + at]] += jnp.dot(
            side, wide_ref[at, :rows], preferred_element_type=F32
        )
    for low in range(sum_ref.shape[0]):
        out_ref[:, low * cols:(low + 1) * cols] = sum_ref[low].astype(BF16)


def make_product(place, order, sides, blocks, lows):
    length, full = sides[0].shape
    cols = blocks[0].shape[1]
    rows = blocks[0].shape[0]
    vmem = pl.BlockSpec(memory_space=pltpu.VMEM)
    return pl.pallas_call(
        functools.partial(product_body, order),
        in_specs=[pl.BlockSpec(memory_space=pltpu.SMEM)]
        + [vmem] * len(sides)
        + [pl.BlockSpec(memory_space=pl.ANY)] * len(blocks),
        out_specs=vmem,
        out_shape=jax.ShapeDtypeStruct((length, lows * cols), BF16),
        scratch_shapes=[
            pltpu.VMEM((len(sides), length, full), BF16),
            pltpu.VMEM((lows, length, cols), F32),
            pltpu.VMEM((len(blocks), rows, cols), BF16),
            pltpu.SemaphoreType.DMA((len(blocks),)),
        ],
        name="product",
    )(place, *near(*sides), *blocks)


def reverse_bits(value, count):
    result = 0
    while count > 1:
        result, value, count = result * 2 + value % 2, value // 2, count // 2
    return result


def cycle_of(highs, lows):
    walk = [(high, 0) for high in range(highs)]
    for at in range(highs - 1, -1, -1):
        lows_at = range(1, lows) if (highs - 1 - at) % 2 == 0 else range(lows - 1, 0, -1)
        walk += [(at, low) for low in lows_at]
    return [high * lows + low for high, low in walk]


def body(
    tokens,
    embedding,
    norm_gain,
    in_weight,
    short_taps,
    decay_rates,
    residue,
    skip_weight,
    out_weight,
):
    ctx_count = lax.axis_size("ctx")
    fsdp_count = lax.axis_size("fsdp")
    lows = ctx_count // fsdp_count
    ctx_at = lax.axis_index("ctx")
    fsdp_at = lax.axis_index("fsdp")
    high_at, low_at = ctx_at // lows, ctx_at % lows
    tok_count = tokens.shape[0]
    _, columns = embedding.shape
    local_channels = in_weight.shape[2]
    part = local_channels // lows
    own = local_channels // ctx_count

    def move(value, target):
        return send(value, ctx_count, fsdp_count, target)

    by_kind = jnp.swapaxes(in_weight, 0, 1)
    weights, ids = [], [tokens[None, :]]
    for shift in range(1, lows):
        def neighbour(i, j):
            return (i // lows * lows + (i % lows - shift) % lows, j)

        going = lax.dynamic_slice_in_dim(by_kind, (low_at - shift) % lows * part, part, 2)
        weights.append(move(going, neighbour))
        ids.append(move(tokens[None, :], neighbour))

    (by_kind,) = after((by_kind,), going)
    weights.insert(0, lax.dynamic_slice_in_dim(by_kind, low_at * part, part, 2))

    chips = fsdp_count // 2
    across = None
    for shift in range(1, chips):
        got = move(
            embedding, lambda i, j: (i, (j + 2 * shift) % fsdp_count) if j == i // lows else None
        )
        across = got if across is None else across + got
    cycle = cycle_of(fsdp_count, lows)
    spot = {ctx: at for at, ctx in enumerate(cycle)}
    moved = move(
        out_weight,
        lambda i, j: ((reverse_bits(j, fsdp_count) ^ i // lows) * lows + i % lows, i // lows),
    )
    ahead, behind = [moved], [moved]
    rounds = (ctx_count - 1) // 2
    steps = [*range(rounds + 1), *range(-1, -rounds - 1, -1), rounds + 1, rounds + 1]
    known = []
    for i in range(ctx_count):
        met = [cycle[(spot[i] - step) % ctx_count] for step in steps]
        for j in range(fsdp_count):
            origin = 0 if j == i // lows else 1 if (j - i // lows) % 2 == 0 else 2
            flips = [reverse_bits(ctx // lows ^ j, fsdp_count) ^ j for ctx in met]
            known.append([i % lows, origin, i, i // lows, *flips, *(ctx % lows for ctx in met)])
    place = jnp.array(known, jnp.int32)[ctx_at * fsdp_count + fsdp_at]

    channel_at = low_at * part + high_at * own
    per_group = min(GROUP, own)
    group_count = own // per_group
    decay = lax.dynamic_slice_in_dim(decay_rates.T, channel_at // GROUP, group_count, 0)
    weight = lax.dynamic_slice_in_dim(residue.T, channel_at // GROUP, group_count, 0)
    taps = lax.dynamic_slice_in_dim(short_taps, channel_at, own, 2)
    taps = taps.reshape(taps.shape[0], 3 * own).T
    skip = lax.dynamic_slice_in_dim(skip_weight, channel_at, own, 0)[:, None]
    gain = lax.dynamic_slice_in_dim(norm_gain, high_at * columns, columns, 0)[None, :]
    filters = make_filters(decay, weight, taps, skip)
    (across,) = after((across,), gain, place, *filters)
    holder = jnp.where(fsdp_at == high_at, embedding, across)
    beside = move(holder, lambda i, j: (i, j ^ 1) if j % 2 == i // lows % 2 else None)

    def turn(*others):
        low, high = after((ahead[-1], behind[-1]), *others)
        ahead.append(move(low, lambda i, j: (cycle[(spot[i] + 1) % ctx_count], j)))
        behind.append(move(high, lambda i, j: (cycle[(spot[i] - 1) % ctx_count], j)))

    turn()
    outgoing = make_table(place, embedding, across, beside, gain, weights, ids, fsdp_count)
    pieces = [outgoing[0]]
    for shift in range(1, fsdp_count):
        pieces.append(
            move(outgoing[shift], lambda i, j: ((i // lows + shift) % fsdp_count * lows + i % lows, j))
        )

    for _ in range(1, rounds - 1):
        pieces = list(after(pieces, ahead[-1], behind[-1]))
        turn(*pieces)
    gated = make_mixer(
        place, columns * fsdp_count, short_taps.shape[0], tok_count, filters, pieces, ctx_count
    )

    pieces = [gated[0]]
    for shift in range(1, ctx_count):
        pieces.append(move(gated[shift], lambda i, j: ((i + shift) % ctx_count, j)))
    pieces = list(after(pieces, ahead[-1], behind[-1]))
    turn(gated[0])
    ordered = make_order(place, pieces, lows)
    middle = out_weight.shape[0] // 2
    low, high = after((ahead[-1], behind[-1]), ordered)
    last_ahead = move(low[:middle], lambda i, j: (cycle[(spot[i] + 1) % ctx_count], j))
    last_behind = move(high[middle:], lambda i, j: (cycle[(spot[i] - 1) % ctx_count], j))
    blocks = ahead + behind[1:] + [last_ahead, last_behind]
    sides, order = [ordered], [0]
    reach = fsdp_count // 2
    while reach:
        more = []
        for side in sides:
            more.append(move(side, lambda i, j: (i, j ^ reach)))
        sides = sides + more
        order = order + [at ^ reach for at in order]
        reach //= 2
    return make_product(place, tuple(order), sides, blocks, lows)


def solution(mesh):
    placed = (
        P("ctx"),
        P(None, "fsdp"),
        P(),
        P("ctx", None, "fsdp"),
        P(None, None, "fsdp"),
        P(None, "fsdp"),
        P(None, "fsdp"),
        P("fsdp"),
        P("fsdp", "ctx"),
    )
    return jax.shard_map(
        body, mesh=mesh, in_specs=placed, out_specs=P("ctx", "fsdp"), check_vma=False
    )
```

```python
import functools

import jax
import jax.numpy as jnp
from jax import lax
from jax.experimental import pallas as pl
from jax.experimental.pallas import tpu as pltpu
from jax.sharding import PartitionSpec as P


GROUP = 16
CHUNK = 256
TILE = 512
EXTRA = 16
PLACES = 4
BASE = 16
AXES = ("ctx", "fsdp")
BF16 = jnp.bfloat16
F32 = jnp.float32


def send(value, ctx_count, fsdp_count, target):
    pairs = []
    for i in range(ctx_count):
        for j in range(fsdp_count):
            to = target(i, j)
            if to is not None:
                pairs.append((i * fsdp_count + j, to[0] * fsdp_count + to[1]))
    return lax.ppermute(value, AXES, pairs)


def after(values, *others):
    return lax.optimization_barrier((tuple(values), others))[0]


def near(*values):
    return [pltpu.with_memory_space_constraint(value, pltpu.VMEM) for value in values]


def split_high_low(value):
    high = value.astype(BF16)
    return high, (value - high.astype(F32)).astype(BF16)


def filter_body(
    decay_ref, residue_ref, decay_col_ref, residue_col_ref, taps_ref, skip_ref,
    near_ref, into_ref, outof_ref, step_ref, side_ref,
):
    count = taps_ref.shape[1]
    side_ref[:, :count] = taps_ref[...]
    side_ref[:skip_ref.shape[0], count:count + 1] = skip_ref[...]
    groups, modes = decay_ref.shape
    rows = lax.broadcasted_iota(jnp.int32, (CHUNK, CHUNK), 0)
    cols = lax.broadcasted_iota(jnp.int32, (CHUNK, CHUNK), 1)
    lag = (cols - rows).astype(F32)
    clipped = jnp.maximum(lag, 0.0)
    back = (CHUNK - 1 - lax.broadcasted_iota(jnp.int32, (CHUNK, modes), 0)).astype(F32)
    ahead = (1 + lax.broadcasted_iota(jnp.int32, (modes, CHUNK), 1)).astype(F32)
    for group in range(groups):
        total = jnp.zeros((CHUNK, CHUNK), F32)
        for mode in range(modes):
            total += residue_ref[group, mode] * jnp.exp(-decay_ref[group, mode] * clipped)
        near_ref[group] = jnp.where(lag >= 0.0, total, 0.0).astype(BF16)
        rate_row = decay_col_ref[group, 0:1, :]
        into_high, into_low = split_high_low(jnp.exp(-rate_row * back))
        into_ref[group] = jnp.concatenate([into_high, into_low], axis=1)
        rate_col = jnp.swapaxes(jnp.broadcast_to(rate_row, (8, modes)), 0, 1)[:, 0:1]
        residue_row = residue_col_ref[group, 0:1, :]
        residue_col = jnp.swapaxes(jnp.broadcast_to(residue_row, (8, modes)), 0, 1)[:, 0:1]
        outof_high, outof_low = split_high_low(residue_col * jnp.exp(-rate_col * ahead))
        outof_ref[group] = jnp.concatenate([outof_high, outof_high, outof_low], axis=0)
        step_ref[group] = jnp.exp(-rate_row * CHUNK)


def make_filters(decay, residue, taps, skip):
    groups, modes = decay.shape
    smem = pl.BlockSpec(memory_space=pltpu.SMEM)
    vmem = pl.BlockSpec(memory_space=pltpu.VMEM)
    return pl.pallas_call(
        filter_body,
        in_specs=[smem, smem] + [vmem] * 4,
        out_specs=[vmem] * 5,
        out_shape=[
            jax.ShapeDtypeStruct((groups, CHUNK, CHUNK), BF16),
            jax.ShapeDtypeStruct((groups, CHUNK, 2 * modes), BF16),
            jax.ShapeDtypeStruct((groups, 3 * modes, CHUNK), BF16),
            jax.ShapeDtypeStruct((groups, 1, modes), F32),
            jax.ShapeDtypeStruct((taps.shape[0], 128), F32),
        ],
        name="filters",
    )(decay, residue, decay[:, None, :], residue[:, None, :], taps, skip)


def table_body(count, place_ref, own_ref, across_ref, beside_ref, gain_ref, *refs):
    raw_ref, scaled_ref, extra_ref, flip_ref = refs[-4:]
    weight_refs, token_refs, out_refs = refs[:count], refs[count:2 * count], refs[2 * count:-4]
    vocab, columns = own_ref.shape
    width = columns // count
    pieces, rows = len(out_refs), out_refs[0].shape[0]
    low_at, origin, high_at = place_ref[0], place_ref[1], place_ref[3]

    @pl.when(origin == 0)
    def _():
        raw_ref[...] = own_ref[...].astype(F32)

    @pl.when(origin == 1)
    def _():
        raw_ref[...] = across_ref[...].astype(F32)

    @pl.when(origin == 2)
    def _():
        raw_ref[...] = beside_ref[...].astype(F32)

    raw = raw_ref[...]
    scaled_ref[...] = (raw * gain_ref[...]).astype(BF16)
    extra_ref[...] = jnp.zeros_like(extra_ref)
    squares = jnp.broadcast_to(jnp.sum(raw * raw, axis=1, keepdims=True), (vocab, 128))
    squares = jnp.swapaxes(squares, 0, 1)[0:1, :]
    for row in range(3):
        rounded = squares.astype(BF16).astype(F32)
        extra_ref[row:row + 1, :] = rounded
        squares = squares - rounded
    for shift, token_ref in enumerate(token_refs):
        low = lax.rem(low_at + shift, count)
        extra_ref[pl.ds(3 + low, 1), :] = (token_ref[...] // BASE).astype(F32)
        extra_ref[pl.ds(3 + count + low, 1), :] = (token_ref[...] % BASE).astype(F32)
    extra = extra_ref[...].astype(BF16)
    each = (rows - EXTRA) // 3
    for out_ref in out_refs:
        out_ref[:EXTRA, :] = extra
    for kind in range(3):
        total = None
        for shift, weight_ref in enumerate(weight_refs):
            start = pl.multiple_of(lax.rem(low_at + shift, count) * width, width)
            part = jnp.dot(scaled_ref[:, pl.ds(start, width)], weight_ref[kind], preferred_element_type=F32)
            total = part if total is None else total + part
        flip_ref[...] = jnp.swapaxes(total, 0, 1)
        for shift, out_ref in enumerate(out_refs):
            start = pl.multiple_of(lax.rem(high_at + shift, pieces) * each, each)
            out_ref[EXTRA + kind * each:EXTRA + (kind + 1) * each, :] = flip_ref[pl.ds(start, each), :].astype(BF16)


def make_table(place, own, across, beside, gain, weights, tokens, pieces):
    vocab = own.shape[0]
    channels = weights[0].shape[2]
    vmem = pl.BlockSpec(memory_space=pltpu.VMEM)
    return pl.pallas_call(
        functools.partial(table_body, len(weights)),
        in_specs=[pl.BlockSpec(memory_space=pltpu.SMEM)] + [vmem] * (4 + len(weights) + len(tokens)),
        out_specs=[vmem] * pieces,
        out_shape=[pltpu.VMEM((EXTRA + 3 * channels // pieces, vocab), BF16)] * pieces,
        scratch_shapes=[
            pltpu.VMEM(own.shape, F32),
            pltpu.VMEM(own.shape, BF16),
            pltpu.VMEM((EXTRA, vocab), F32),
            pltpu.VMEM((channels, vocab), F32),
        ],
        name="table",
    )(place, own, across, beside, gain, *weights, *tokens)


def mixer_body(width, taps, place_ref, near_ref, into_ref, outof_ref, step_ref, taps_ref, *refs):
    query_ref, drive_ref, conv_ref, token_ref, stage_ref = refs[-5:]
    ctx_at = place_ref[2]
    out_refs = refs[-5 - token_ref.shape[0]:-5]
    piece_refs = refs[:-5 - token_ref.shape[0]]
    rows, vocab = piece_refs[0].shape
    rows -= EXTRA
    channels = rows // 3
    blocks, _, block = token_ref.shape
    length = blocks * block
    count = len(piece_refs)
    lows = blocks // count
    total = None
    squares = None
    for shift, ref in enumerate(piece_refs):
        head = ref[:EXTRA, :].astype(F32)
        summed = head[0:1] + head[1:2] + head[2:3]
        squares = summed if squares is None else squares + summed
        high = lax.rem(ctx_at // lows - shift + count, count)
        for low in range(lows):
            ids = head[3 + low:4 + low] * BASE + head[3 + lows + low:4 + lows + low]
            token_ref[high * lows + low] = ids[:, :block].astype(jnp.int32)
        part = ref[EXTRA:, :].astype(F32)
        total = part if total is None else total + part
    table = (total * lax.rsqrt(squares * (1.0 / width) + 1e-05)).astype(BF16)
    ids = lax.broadcasted_iota(jnp.int32, (vocab, TILE), 0)
    halo = jnp.zeros((rows, 128), F32)
    for tile in range(length // TILE):
        at = tile * TILE
        inside = at % block
        tokens = token_ref[at // block][:, inside:inside + TILE]
        hot = jnp.where(ids == tokens, 1.0, 0.0).astype(BF16)
        projected = jnp.dot(table, hot, preferred_element_type=F32)
        extended = jnp.concatenate([halo, projected], axis=1)
        halo = projected[:, TILE - 128:]
        short = taps_ref[:, 0:1] * projected
        for lag in range(1, taps):
            short += taps_ref[:, lag:lag + 1] * pltpu.roll(extended, lag, 1)[:, 128:]
        query_ref[:, at:at + TILE] = short[:channels]
        drive_ref[:, at:at + TILE] = short[channels:2 * channels] * short[2 * channels:]
    groups = near_ref.shape[0]
    per = channels // groups
    modes = step_ref.shape[2]
    chunks = length // CHUNK
    for group in range(groups):
        base = group * per
        stacked = jnp.concatenate(
            [drive_ref[base:base + per, n * CHUNK:(n + 1) * CHUNK] for n in range(chunks)], axis=0
        ).astype(BF16)
        both = jnp.dot(stacked, into_ref[group], preferred_element_type=F32)
        ends = both[:, :modes] + both[:, modes:]
        step = step_ref[group]
        state = jnp.zeros((per, modes), F32)
        starts = []
        for n in range(chunks):
            starts.append(state)
            state = state * step + ends[n * per:(n + 1) * per]
        high, low = split_high_low(jnp.concatenate(starts, axis=0))
        conv_ref[...] = jnp.dot(stacked, near_ref[group], preferred_element_type=F32) + jnp.dot(
            jnp.concatenate([high, low, high], axis=1), outof_ref[group], preferred_element_type=F32
        )
        for n in range(chunks):
            here = slice(n * CHUNK, (n + 1) * CHUNK)
            response = conv_ref[n * per:(n + 1) * per, :] + taps_ref[base:base + per, taps:taps + 1] * drive_ref[base:base + per, here]
            at = n * CHUNK
            stage_ref[at // block, base:base + per, at % block:at % block + CHUNK] = (
                query_ref[base:base + per, here] * response
            ).astype(BF16)
    for shift, out_ref in enumerate(out_refs):
        out_ref[...] = stage_ref[lax.rem(ctx_at + shift, blocks)]


def make_mixer(place, width, taps, block, filters, pieces, blocks):
    rows = pieces[0].shape[0] - EXTRA
    channels = rows // 3
    length = block * blocks
    groups = filters[0].shape[0]
    vmem = pl.BlockSpec(memory_space=pltpu.VMEM)
    return pl.pallas_call(
        functools.partial(mixer_body, width, taps),
        in_specs=[pl.BlockSpec(memory_space=pltpu.SMEM)] + [vmem] * (5 + len(pieces)),
        out_specs=[vmem] * blocks,
        out_shape=[pltpu.VMEM((channels, block), BF16)] * blocks,
        scratch_shapes=[
            pltpu.VMEM((channels, length), F32),
            pltpu.VMEM((channels, length), F32),
            pltpu.VMEM((length // CHUNK * (channels // groups), CHUNK), F32),
            pltpu.VMEM((blocks, 1, block), jnp.int32),
            pltpu.VMEM((blocks, channels, block), BF16),
        ],
        name="mixer",
    )(place, *filters, *near(*pieces))


def order_body(lows, place_ref, *refs):
    piece_refs, out_ref, stage_ref = refs[:-2], refs[-2], refs[-1]
    count = len(piece_refs)
    rows = piece_refs[0].shape[0]
    for shift, ref in enumerate(piece_refs):
        source = lax.rem(place_ref[2] - shift + count, count)
        start = pl.multiple_of((lax.rem(source, lows) * (count // lows) + source // lows) * rows, rows)
        stage_ref[pl.ds(start, rows), :] = ref[...].astype(F32)
    out_ref[...] = jnp.swapaxes(stage_ref[...], 0, 1).astype(BF16)


def make_order(place, pieces, lows):
    rows, length = pieces[0].shape
    vmem = pl.BlockSpec(memory_space=pltpu.VMEM)
    return pl.pallas_call(
        functools.partial(order_body, lows),
        in_specs=[pl.BlockSpec(memory_space=pltpu.SMEM)] + [vmem] * len(pieces),
        out_specs=vmem,
        out_shape=pltpu.VMEM((length, rows * len(pieces)), BF16),
        scratch_shapes=[pltpu.VMEM((rows * len(pieces), length), F32)],
        name="order",
    )(place, *near(*pieces))


def product_body(order, place_ref, *refs):
    side_refs = refs[:len(order)]
    out_ref, sides_ref, wide_ref, arrived = refs[-4:]
    block_refs = refs[len(order):-4]
    count = len(block_refs)
    full, cols = block_refs[0].shape
    copies = []
    for at, ref in enumerate(block_refs):
        first = full // 2 if at == count - 1 else 0
        start = pl.multiple_of(place_ref[PLACES + at] * full + first, full // 2)
        copies.append(
            pltpu.make_async_copy(
                ref,
                wide_ref.at[place_ref[PLACES + count + at], pl.ds(start, ref.shape[0])],
                arrived.at[at],
            )
        )
        copies[-1].start()
    for flip, ref in zip(order, side_refs):
        sides_ref[:, flip * full:(flip + 1) * full] = ref[...]
    for copy in copies:
        copy.wait()
    for low in range(wide_ref.shape[0]):
        out_ref[:, low * cols:(low + 1) * cols] = jnp.dot(
            sides_ref[...], wide_ref[low], preferred_element_type=F32
        ).astype(BF16)


def make_product(place, order, sides, blocks, lows):
    length, full = sides[0].shape
    cols = blocks[0].shape[1]
    rows = blocks[0].shape[0]
    vmem = pl.BlockSpec(memory_space=pltpu.VMEM)
    return pl.pallas_call(
        functools.partial(product_body, order),
        in_specs=[pl.BlockSpec(memory_space=pltpu.SMEM)]
        + [vmem] * len(sides)
        + [pl.BlockSpec(memory_space=pl.ANY)] * len(blocks),
        out_specs=vmem,
        out_shape=jax.ShapeDtypeStruct((length, lows * cols), BF16),
        scratch_shapes=[
            pltpu.VMEM((length, len(sides) * full), BF16),
            pltpu.VMEM((lows, len(sides) * rows, cols), BF16),
            pltpu.SemaphoreType.DMA((len(blocks),)),
        ],
        name="product",
    )(place, *near(*sides), *blocks)


def reverse_bits(value, count):
    result = 0
    while count > 1:
        result, value, count = result * 2 + value % 2, value // 2, count // 2
    return result


def cycle_of(highs, lows):
    walk = [(high, 0) for high in range(highs)]
    for at in range(highs - 1, -1, -1):
        lows_at = range(1, lows) if (highs - 1 - at) % 2 == 0 else range(lows - 1, 0, -1)
        walk += [(at, low) for low in lows_at]
    return [high * lows + low for high, low in walk]


def body(
    tokens,
    embedding,
    norm_gain,
    in_weight,
    short_taps,
    decay_rates,
    residue,
    skip_weight,
    out_weight,
):
    ctx_count = lax.axis_size("ctx")
    fsdp_count = lax.axis_size("fsdp")
    lows = ctx_count // fsdp_count
    ctx_at = lax.axis_index("ctx")
    fsdp_at = lax.axis_index("fsdp")
    high_at, low_at = ctx_at // lows, ctx_at % lows
    tok_count = tokens.shape[0]
    _, columns = embedding.shape
    local_channels = in_weight.shape[2]
    part = local_channels // lows
    own = local_channels // ctx_count

    def move(value, target):
        return send(value, ctx_count, fsdp_count, target)

    by_kind = jnp.swapaxes(in_weight, 0, 1)
    weights, ids = [], [tokens[None, :]]
    for shift in range(1, lows):
        def neighbour(i, j):
            return (i // lows * lows + (i % lows - shift) % lows, j)

        going = lax.dynamic_slice_in_dim(by_kind, (low_at - shift) % lows * part, part, 2)
        weights.append(move(going, neighbour))
        ids.append(move(tokens[None, :], neighbour))

    (by_kind,) = after((by_kind,), going)
    weights.insert(0, lax.dynamic_slice_in_dim(by_kind, low_at * part, part, 2))

    chips = fsdp_count // 2
    across = None
    for shift in range(1, chips):
        got = move(
            embedding, lambda i, j: (i, (j + 2 * shift) % fsdp_count) if j == i // lows else None
        )
        across = got if across is None else across + got
    cycle = cycle_of(fsdp_count, lows)
    spot = {ctx: at for at, ctx in enumerate(cycle)}
    moved = move(
        out_weight,
        lambda i, j: ((reverse_bits(j, fsdp_count) ^ i // lows) * lows + i % lows, i // lows),
    )
    ahead, behind = [moved], [moved]
    rounds = (ctx_count - 1) // 2
    steps = [*range(rounds + 1), *range(-1, -rounds - 1, -1), rounds + 1, rounds + 1]
    known = []
    for i in range(ctx_count):
        met = [cycle[(spot[i] - step) % ctx_count] for step in steps]
        for j in range(fsdp_count):
            origin = 0 if j == i // lows else 1 if (j - i // lows) % 2 == 0 else 2
            flips = [reverse_bits(ctx // lows ^ j, fsdp_count) ^ j for ctx in met]
            known.append([i % lows, origin, i, i // lows, *flips, *(ctx % lows for ctx in met)])
    place = jnp.array(known, jnp.int32)[ctx_at * fsdp_count + fsdp_at]

    channel_at = low_at * part + high_at * own
    per_group = min(GROUP, own)
    group_count = own // per_group
    decay = lax.dynamic_slice_in_dim(decay_rates.T, channel_at // GROUP, group_count, 0)
    weight = lax.dynamic_slice_in_dim(residue.T, channel_at // GROUP, group_count, 0)
    taps = lax.dynamic_slice_in_dim(short_taps, channel_at, own, 2)
    taps = taps.reshape(taps.shape[0], 3 * own).T
    skip = lax.dynamic_slice_in_dim(skip_weight, channel_at, own, 0)[:, None]
    gain = lax.dynamic_slice_in_dim(norm_gain, high_at * columns, columns, 0)[None, :]
    (across,) = after((across,), gain, place, weights[0])
    holder = jnp.where(fsdp_at == high_at, embedding, across)
    beside = move(holder, lambda i, j: (i, j ^ 1) if j % 2 == i // lows % 2 else None)

    def turn(*others):
        low, high = after((ahead[-1], behind[-1]), *others)
        ahead.append(move(low, lambda i, j: (cycle[(spot[i] + 1) % ctx_count], j)))
        behind.append(move(high, lambda i, j: (cycle[(spot[i] - 1) % ctx_count], j)))

    turn()
    outgoing = make_table(place, embedding, across, beside, gain, weights, ids, fsdp_count)
    pieces = [outgoing[0]]
    for shift in range(1, fsdp_count):
        pieces.append(
            move(outgoing[shift], lambda i, j: ((i // lows + shift) % fsdp_count * lows + i % lows, j))
        )

    filters = make_filters(*after((decay, weight, taps, skip), *outgoing))
    for _ in range(1, rounds - 1):
        pieces = list(after(pieces, ahead[-1], behind[-1]))
        turn(*pieces)
    gated = make_mixer(
        place, columns * fsdp_count, short_taps.shape[0], tok_count, filters, pieces, ctx_count
    )

    pieces = [gated[0]]
    for shift in range(1, ctx_count):
        pieces.append(move(gated[shift], lambda i, j: ((i + shift) % ctx_count, j)))
    pieces = list(after(pieces, ahead[-1], behind[-1]))
    turn(gated[0])
    ordered = make_order(place, pieces, lows)
    middle = out_weight.shape[0] // 2
    low, high = after((ahead[-1], behind[-1]), ordered)
    last_ahead = move(low[:middle], lambda i, j: (cycle[(spot[i] + 1) % ctx_count], j))
    last_behind = move(high[middle:], lambda i, j: (cycle[(spot[i] - 1) % ctx_count], j))
    blocks = ahead + behind[1:] + [last_ahead, last_behind]
    sides, order = [ordered], [0]
    reach = fsdp_count // 2
    while reach:
        more = []
        for side in sides:
            more.append(move(side, lambda i, j: (i, j ^ reach)))
        sides = sides + more
        order = order + [at ^ reach for at in order]
        reach //= 2
    return make_product(place, tuple(order), sides, blocks, lows)


def solution(mesh):
    placed = (
        P("ctx"),
        P(None, "fsdp"),
        P(),
        P("ctx", None, "fsdp"),
        P(None, None, "fsdp"),
        P(None, "fsdp"),
        P(None, "fsdp"),
        P("fsdp"),
        P("fsdp", "ctx"),
    )
    return jax.shard_map(
        body, mesh=mesh, in_specs=placed, out_specs=P("ctx", "fsdp"), check_vma=False
    )
```

```python
import functools

import jax
import jax.numpy as jnp
from jax import lax
from jax.experimental import pallas as pl
from jax.experimental.pallas import tpu as pltpu
from jax.sharding import PartitionSpec as P


GROUP = 16
CHUNK = 256
TILE = 512
EXTRA = 16
PLACES = 4
BASE = 16
AXES = ("ctx", "fsdp")
BF16 = jnp.bfloat16
F32 = jnp.float32


def send(value, ctx_count, fsdp_count, target):
    pairs = []
    for i in range(ctx_count):
        for j in range(fsdp_count):
            to = target(i, j)
            if to is not None:
                pairs.append((i * fsdp_count + j, to[0] * fsdp_count + to[1]))
    return lax.ppermute(value, AXES, pairs)


def after(values, *others):
    return lax.optimization_barrier((tuple(values), others))[0]


def near(*values):
    return [pltpu.with_memory_space_constraint(value, pltpu.VMEM) for value in values]


def split_high_low(value):
    high = value.astype(BF16)
    return high, (value - high.astype(F32)).astype(BF16)


def filter_body(
    decay_ref, residue_ref, decay_col_ref, residue_col_ref, taps_ref, skip_ref,
    near_ref, into_ref, outof_ref, step_ref, side_ref,
):
    count = taps_ref.shape[1]
    side_ref[:, :count] = taps_ref[...]
    side_ref[:skip_ref.shape[0], count:count + 1] = skip_ref[...]
    groups, modes = decay_ref.shape
    rows = lax.broadcasted_iota(jnp.int32, (CHUNK, CHUNK), 0)
    cols = lax.broadcasted_iota(jnp.int32, (CHUNK, CHUNK), 1)
    lag = (cols - rows).astype(F32)
    clipped = jnp.maximum(lag, 0.0)
    back = (CHUNK - 1 - lax.broadcasted_iota(jnp.int32, (CHUNK, modes), 0)).astype(F32)
    ahead = (1 + lax.broadcasted_iota(jnp.int32, (modes, CHUNK), 1)).astype(F32)
    for group in range(groups):
        total = jnp.zeros((CHUNK, CHUNK), F32)
        for mode in range(modes):
            total += residue_ref[group, mode] * jnp.exp(-decay_ref[group, mode] * clipped)
        near_ref[group] = jnp.where(lag >= 0.0, total, 0.0).astype(BF16)
        rate_row = decay_col_ref[group, 0:1, :]
        into_high, into_low = split_high_low(jnp.exp(-rate_row * back))
        into_ref[group] = jnp.concatenate([into_high, into_low], axis=1)
        rate_col = jnp.swapaxes(jnp.broadcast_to(rate_row, (8, modes)), 0, 1)[:, 0:1]
        residue_row = residue_col_ref[group, 0:1, :]
        residue_col = jnp.swapaxes(jnp.broadcast_to(residue_row, (8, modes)), 0, 1)[:, 0:1]
        outof_high, outof_low = split_high_low(residue_col * jnp.exp(-rate_col * ahead))
        outof_ref[group] = jnp.concatenate([outof_high, outof_high, outof_low], axis=0)
        step_ref[group] = jnp.exp(-rate_row * CHUNK)


def make_filters(decay, residue, taps, skip):
    groups, modes = decay.shape
    smem = pl.BlockSpec(memory_space=pltpu.SMEM)
    vmem = pl.BlockSpec(memory_space=pltpu.VMEM)
    return pl.pallas_call(
        filter_body,
        in_specs=[smem, smem] + [vmem] * 4,
        out_specs=[vmem] * 5,
        out_shape=[
            jax.ShapeDtypeStruct((groups, CHUNK, CHUNK), BF16),
            jax.ShapeDtypeStruct((groups, CHUNK, 2 * modes), BF16),
            jax.ShapeDtypeStruct((groups, 3 * modes, CHUNK), BF16),
            jax.ShapeDtypeStruct((groups, 1, modes), F32),
            jax.ShapeDtypeStruct((taps.shape[0], 128), F32),
        ],
        name="filters",
    )(decay, residue, decay[:, None, :], residue[:, None, :], taps, skip)


def table_body(count, place_ref, own_ref, across_ref, beside_ref, gain_ref, *refs):
    raw_ref, scaled_ref, extra_ref, flip_ref = refs[-4:]
    weight_refs, token_refs, out_refs = refs[:count], refs[count:2 * count], refs[2 * count:-4]
    vocab, columns = own_ref.shape
    width = columns // count
    pieces, rows = len(out_refs), out_refs[0].shape[0]
    low_at, origin, high_at = place_ref[0], place_ref[1], place_ref[3]

    @pl.when(origin == 0)
    def _():
        raw_ref[...] = own_ref[...].astype(F32)

    @pl.when(origin == 1)
    def _():
        raw_ref[...] = across_ref[...].astype(F32)

    @pl.when(origin == 2)
    def _():
        raw_ref[...] = beside_ref[...].astype(F32)

    raw = raw_ref[...]
    scaled_ref[...] = (raw * gain_ref[...]).astype(BF16)
    extra_ref[...] = jnp.zeros_like(extra_ref)
    squares = jnp.broadcast_to(jnp.sum(raw * raw, axis=1, keepdims=True), (vocab, 128))
    squares = jnp.swapaxes(squares, 0, 1)[0:1, :]
    for row in range(3):
        rounded = squares.astype(BF16).astype(F32)
        extra_ref[row:row + 1, :] = rounded
        squares = squares - rounded
    for shift, token_ref in enumerate(token_refs):
        low = lax.rem(low_at + shift, count)
        extra_ref[pl.ds(3 + low, 1), :] = (token_ref[...] // BASE).astype(F32)
        extra_ref[pl.ds(3 + count + low, 1), :] = (token_ref[...] % BASE).astype(F32)
    extra = extra_ref[...].astype(BF16)
    each = (rows - EXTRA) // 3
    for out_ref in out_refs:
        out_ref[:EXTRA, :] = extra
    for kind in range(3):
        total = None
        for shift, weight_ref in enumerate(weight_refs):
            start = pl.multiple_of(lax.rem(low_at + shift, count) * width, width)
            part = jnp.dot(scaled_ref[:, pl.ds(start, width)], weight_ref[kind], preferred_element_type=F32)
            total = part if total is None else total + part
        flip_ref[...] = jnp.swapaxes(total, 0, 1)
        for shift, out_ref in enumerate(out_refs):
            start = pl.multiple_of(lax.rem(high_at + shift, pieces) * each, each)
            out_ref[EXTRA + kind * each:EXTRA + (kind + 1) * each, :] = flip_ref[pl.ds(start, each), :].astype(BF16)


def make_table(place, own, across, beside, gain, weights, tokens, pieces):
    vocab = own.shape[0]
    channels = weights[0].shape[2]
    vmem = pl.BlockSpec(memory_space=pltpu.VMEM)
    return pl.pallas_call(
        functools.partial(table_body, len(weights)),
        in_specs=[pl.BlockSpec(memory_space=pltpu.SMEM)] + [vmem] * (4 + len(weights) + len(tokens)),
        out_specs=[vmem] * pieces,
        out_shape=[pltpu.VMEM((EXTRA + 3 * channels // pieces, vocab), BF16)] * pieces,
        scratch_shapes=[
            pltpu.VMEM(own.shape, F32),
            pltpu.VMEM(own.shape, BF16),
            pltpu.VMEM((EXTRA, vocab), F32),
            pltpu.VMEM((channels, vocab), F32),
        ],
        name="table",
    )(place, own, across, beside, gain, *weights, *tokens)


def mixer_body(width, taps, place_ref, near_ref, into_ref, outof_ref, step_ref, taps_ref, *refs):
    query_ref, drive_ref, conv_ref, token_ref, stage_ref, found_ref, tap_ref = refs[-7:]
    ctx_at = place_ref[2]
    out_refs = refs[-7 - token_ref.shape[0]:-7]
    piece_refs = refs[:-7 - token_ref.shape[0]]
    rows, vocab = piece_refs[0].shape
    rows -= EXTRA
    channels = rows // 3
    blocks, _, block = token_ref.shape
    length = blocks * block
    count = len(piece_refs)
    lows = blocks // count
    total = None
    squares = None
    for shift, ref in enumerate(piece_refs):
        head = ref[:EXTRA, :].astype(F32)
        summed = head[0:1] + head[1:2] + head[2:3]
        squares = summed if squares is None else squares + summed
        high = lax.rem(ctx_at // lows - shift + count, count)
        for low in range(lows):
            ids = head[3 + low:4 + low] * BASE + head[3 + lows + low:4 + lows + low]
            token_ref[high * lows + low] = ids[:, :block].astype(jnp.int32)
        part = ref[EXTRA:, :].astype(F32)
        total = part if total is None else total + part
    table = (total * lax.rsqrt(squares * (1.0 / width) + 1e-05)).astype(BF16)
    for lag in range(taps):
        tap_ref[lag] = jnp.broadcast_to(taps_ref[:rows, lag:lag + 1], (rows, 128))
    ids = lax.broadcasted_iota(jnp.int32, (vocab, TILE), 0)
    wide = TILE // 128
    tiles = length // TILE

    def look_up(tile):
        at = tile * TILE
        inside = at % block
        tokens = token_ref[at // block][:, inside:inside + TILE]
        hot = jnp.where(ids == tokens, 1.0, 0.0).astype(BF16)
        here_ref = found_ref.at[tile % 2]
        if tile == 0:
            here_ref[:, :128] = jnp.zeros((rows, 128), F32)
        else:
            here_ref[:, :128] = found_ref[(tile - 1) % 2, :, TILE:]
        here_ref[:, 128:] = jnp.dot(table, hot, preferred_element_type=F32)

    def combine(tile, row):
        extended = found_ref[tile % 2, row:row + 8, :]
        short = None
        for lag in range(taps):
            moved = (pltpu.roll(extended, lag, 1) if lag else extended)[:, 128:]
            term = jnp.concatenate([tap_ref[lag, row:row + 8]] * wide, axis=1) * moved
            short = term if short is None else short + term
        return short

    for tile in range(tiles):
        look_up(tile)
        at = tile * TILE
        for row in range(0, channels, 8):
            query_ref[row:row + 8, at:at + TILE] = combine(tile, row)
            drive_ref[row:row + 8, at:at + TILE] = combine(tile, channels + row) * combine(tile, 2 * channels + row)
    groups = near_ref.shape[0]
    per = channels // groups
    modes = step_ref.shape[2]
    chunks = length // CHUNK
    for group in range(groups):
        base = group * per
        stacked = jnp.concatenate(
            [drive_ref[base:base + per, n * CHUNK:(n + 1) * CHUNK] for n in range(chunks)], axis=0
        ).astype(BF16)
        both = jnp.dot(stacked, into_ref[group], preferred_element_type=F32)
        ends = both[:, :modes] + both[:, modes:]
        step = step_ref[group]
        state = jnp.zeros((per, modes), F32)
        starts = []
        for n in range(chunks):
            starts.append(state)
            state = state * step + ends[n * per:(n + 1) * per]
        high, low = split_high_low(jnp.concatenate(starts, axis=0))
        conv_ref[...] = jnp.dot(stacked, near_ref[group], preferred_element_type=F32) + jnp.dot(
            jnp.concatenate([high, low, high], axis=1), outof_ref[group], preferred_element_type=F32
        )
        for n in range(chunks):
            here = slice(n * CHUNK, (n + 1) * CHUNK)
            response = conv_ref[n * per:(n + 1) * per, :] + taps_ref[base:base + per, taps:taps + 1] * drive_ref[base:base + per, here]
            at = n * CHUNK
            stage_ref[at // block, base:base + per, at % block:at % block + CHUNK] = (
                query_ref[base:base + per, here] * response
            ).astype(BF16)
    for shift, out_ref in enumerate(out_refs):
        out_ref[...] = stage_ref[lax.rem(ctx_at + shift, blocks)]


def make_mixer(place, width, taps, block, filters, pieces, blocks):
    rows = pieces[0].shape[0] - EXTRA
    channels = rows // 3
    length = block * blocks
    groups = filters[0].shape[0]
    vmem = pl.BlockSpec(memory_space=pltpu.VMEM)
    return pl.pallas_call(
        functools.partial(mixer_body, width, taps),
        in_specs=[pl.BlockSpec(memory_space=pltpu.SMEM)] + [vmem] * (5 + len(pieces)),
        out_specs=[vmem] * blocks,
        out_shape=[pltpu.VMEM((channels, block), BF16)] * blocks,
        scratch_shapes=[
            pltpu.VMEM((channels, length), F32),
            pltpu.VMEM((channels, length), F32),
            pltpu.VMEM((length // CHUNK * (channels // groups), CHUNK), F32),
            pltpu.VMEM((blocks, 1, block), jnp.int32),
            pltpu.VMEM((blocks, channels, block), BF16),
            pltpu.VMEM((2, rows, TILE + 128), F32),
            pltpu.VMEM((taps, rows, 128), F32),
        ],
        name="mixer",
    )(place, *filters, *near(*pieces))


def order_body(lows, place_ref, *refs):
    piece_refs, out_ref, stage_ref = refs[:-2], refs[-2], refs[-1]
    count = len(piece_refs)
    rows = piece_refs[0].shape[0]
    for shift, ref in enumerate(piece_refs):
        source = lax.rem(place_ref[2] - shift + count, count)
        start = pl.multiple_of((lax.rem(source, lows) * (count // lows) + source // lows) * rows, rows)
        stage_ref[pl.ds(start, rows), :] = ref[...].astype(F32)
    out_ref[...] = jnp.swapaxes(stage_ref[...], 0, 1).astype(BF16)


def make_order(place, pieces, lows):
    rows, length = pieces[0].shape
    vmem = pl.BlockSpec(memory_space=pltpu.VMEM)
    return pl.pallas_call(
        functools.partial(order_body, lows),
        in_specs=[pl.BlockSpec(memory_space=pltpu.SMEM)] + [vmem] * len(pieces),
        out_specs=vmem,
        out_shape=pltpu.VMEM((length, rows * len(pieces)), BF16),
        scratch_shapes=[pltpu.VMEM((rows * len(pieces), length), F32)],
        name="order",
    )(place, *near(*pieces))


def product_body(order, place_ref, *refs):
    side_refs = refs[:len(order)]
    out_ref, sides_ref, wide_ref, arrived = refs[-4:]
    block_refs = refs[len(order):-4]
    count = len(block_refs)
    full, cols = block_refs[0].shape
    copies = []
    for at, ref in enumerate(block_refs):
        first = full // 2 if at == count - 1 else 0
        start = pl.multiple_of(place_ref[PLACES + at] * full + first, full // 2)
        copies.append(
            pltpu.make_async_copy(
                ref,
                wide_ref.at[place_ref[PLACES + count + at], pl.ds(start, ref.shape[0])],
                arrived.at[at],
            )
        )
        copies[-1].start()
    for flip, ref in zip(order, side_refs):
        sides_ref[:, flip * full:(flip + 1) * full] = ref[...]
    for copy in copies:
        copy.wait()
    for low in range(wide_ref.shape[0]):
        out_ref[:, low * cols:(low + 1) * cols] = jnp.dot(
            sides_ref[...], wide_ref[low], preferred_element_type=F32
        ).astype(BF16)


def make_product(place, order, sides, blocks, lows):
    length, full = sides[0].shape
    cols = blocks[0].shape[1]
    rows = blocks[0].shape[0]
    vmem = pl.BlockSpec(memory_space=pltpu.VMEM)
    return pl.pallas_call(
        functools.partial(product_body, order),
        in_specs=[pl.BlockSpec(memory_space=pltpu.SMEM)]
        + [vmem] * len(sides)
        + [pl.BlockSpec(memory_space=pl.ANY)] * len(blocks),
        out_specs=vmem,
        out_shape=jax.ShapeDtypeStruct((length, lows * cols), BF16),
        scratch_shapes=[
            pltpu.VMEM((length, len(sides) * full), BF16),
            pltpu.VMEM((lows, len(sides) * rows, cols), BF16),
            pltpu.SemaphoreType.DMA((len(blocks),)),
        ],
        name="product",
    )(place, *near(*sides), *blocks)


def reverse_bits(value, count):
    result = 0
    while count > 1:
        result, value, count = result * 2 + value % 2, value // 2, count // 2
    return result


def cycle_of(highs, lows):
    walk = [(high, 0) for high in range(highs)]
    for at in range(highs - 1, -1, -1):
        lows_at = range(1, lows) if (highs - 1 - at) % 2 == 0 else range(lows - 1, 0, -1)
        walk += [(at, low) for low in lows_at]
    return [high * lows + low for high, low in walk]


def body(
    tokens,
    embedding,
    norm_gain,
    in_weight,
    short_taps,
    decay_rates,
    residue,
    skip_weight,
    out_weight,
):
    ctx_count = lax.axis_size("ctx")
    fsdp_count = lax.axis_size("fsdp")
    lows = ctx_count // fsdp_count
    ctx_at = lax.axis_index("ctx")
    fsdp_at = lax.axis_index("fsdp")
    high_at, low_at = ctx_at // lows, ctx_at % lows
    tok_count = tokens.shape[0]
    _, columns = embedding.shape
    local_channels = in_weight.shape[2]
    part = local_channels // lows
    own = local_channels // ctx_count

    def move(value, target):
        return send(value, ctx_count, fsdp_count, target)

    by_kind = jnp.swapaxes(in_weight, 0, 1)
    weights, ids = [], [tokens[None, :]]
    for shift in range(1, lows):
        def neighbour(i, j):
            return (i // lows * lows + (i % lows - shift) % lows, j)

        going = lax.dynamic_slice_in_dim(by_kind, (low_at - shift) % lows * part, part, 2)
        weights.append(move(going, neighbour))
        ids.append(move(tokens[None, :], neighbour))

    (by_kind,) = after((by_kind,), going)
    weights.insert(0, lax.dynamic_slice_in_dim(by_kind, low_at * part, part, 2))

    chips = fsdp_count // 2
    across = None
    for shift in range(1, chips):
        got = move(
            embedding, lambda i, j: (i, (j + 2 * shift) % fsdp_count) if j == i // lows else None
        )
        across = got if across is None else across + got
    cycle = cycle_of(fsdp_count, lows)
    spot = {ctx: at for at, ctx in enumerate(cycle)}
    moved = move(
        out_weight,
        lambda i, j: ((reverse_bits(j, fsdp_count) ^ i // lows) * lows + i % lows, i // lows),
    )
    ahead, behind = [moved], [moved]
    rounds = (ctx_count - 1) // 2
    steps = [*range(rounds + 1), *range(-1, -rounds - 1, -1), rounds + 1, rounds + 1]
    known = []
    for i in range(ctx_count):
        met = [cycle[(spot[i] - step) % ctx_count] for step in steps]
        for j in range(fsdp_count):
            origin = 0 if j == i // lows else 1 if (j - i // lows) % 2 == 0 else 2
            flips = [reverse_bits(ctx // lows ^ j, fsdp_count) ^ j for ctx in met]
            known.append([i % lows, origin, i, i // lows, *flips, *(ctx % lows for ctx in met)])
    place = jnp.array(known, jnp.int32)[ctx_at * fsdp_count + fsdp_at]

    channel_at = low_at * part + high_at * own
    per_group = min(GROUP, own)
    group_count = own // per_group
    decay = lax.dynamic_slice_in_dim(decay_rates.T, channel_at // GROUP, group_count, 0)
    weight = lax.dynamic_slice_in_dim(residue.T, channel_at // GROUP, group_count, 0)
    taps = lax.dynamic_slice_in_dim(short_taps, channel_at, own, 2)
    taps = taps.reshape(taps.shape[0], 3 * own).T
    skip = lax.dynamic_slice_in_dim(skip_weight, channel_at, own, 0)[:, None]
    gain = lax.dynamic_slice_in_dim(norm_gain, high_at * columns, columns, 0)[None, :]
    (across,) = after((across,), gain, place, weights[0])
    holder = jnp.where(fsdp_at == high_at, embedding, across)
    beside = move(holder, lambda i, j: (i, j ^ 1) if j % 2 == i // lows % 2 else None)

    def turn(*others):
        low, high = after((ahead[-1], behind[-1]), *others)
        ahead.append(move(low, lambda i, j: (cycle[(spot[i] + 1) % ctx_count], j)))
        behind.append(move(high, lambda i, j: (cycle[(spot[i] - 1) % ctx_count], j)))

    turn()
    outgoing = make_table(place, embedding, across, beside, gain, weights, ids, fsdp_count)
    pieces = [outgoing[0]]
    for shift in range(1, fsdp_count):
        pieces.append(
            move(outgoing[shift], lambda i, j: ((i // lows + shift) % fsdp_count * lows + i % lows, j))
        )

    filters = make_filters(*after((decay, weight, taps, skip), *outgoing))
    for _ in range(1, rounds - 1):
        pieces = list(after(pieces, ahead[-1], behind[-1]))
        turn(*pieces)
    gated = make_mixer(
        place, columns * fsdp_count, short_taps.shape[0], tok_count, filters, pieces, ctx_count
    )

    pieces = [gated[0]]
    for shift in range(1, ctx_count):
        pieces.append(move(gated[shift], lambda i, j: ((i + shift) % ctx_count, j)))
    pieces = list(after(pieces, ahead[-1], behind[-1]))
    turn(gated[0])
    ordered = make_order(place, pieces, lows)
    middle = out_weight.shape[0] // 2
    low, high = after((ahead[-1], behind[-1]), ordered)
    last_ahead = move(low[:middle], lambda i, j: (cycle[(spot[i] + 1) % ctx_count], j))
    last_behind = move(high[middle:], lambda i, j: (cycle[(spot[i] - 1) % ctx_count], j))
    blocks = ahead + behind[1:] + [last_ahead, last_behind]
    sides, order = [ordered], [0]
    reach = fsdp_count // 2
    while reach:
        more = []
        for side in sides:
            more.append(move(side, lambda i, j: (i, j ^ reach)))
        sides = sides + more
        order = order + [at ^ reach for at in order]
        reach //= 2
    return make_product(place, tuple(order), sides, blocks, lows)


def solution(mesh):
    placed = (
        P("ctx"),
        P(None, "fsdp"),
        P(),
        P("ctx", None, "fsdp"),
        P(None, None, "fsdp"),
        P(None, "fsdp"),
        P(None, "fsdp"),
        P("fsdp"),
        P("fsdp", "ctx"),
    )
    return jax.shard_map(
        body, mesh=mesh, in_specs=placed, out_specs=P("ctx", "fsdp"), check_vma=False
    )
```

```python
import functools

import jax
import jax.numpy as jnp
from jax import lax
from jax.experimental import pallas as pl
from jax.experimental.pallas import tpu as pltpu
from jax.sharding import PartitionSpec as P


GROUP = 16
CHUNK = 256
TILE = 512
EXTRA = 16
PLACES = 4
STRIP = 128
BASE = 16
AXES = ("ctx", "fsdp")
BF16 = jnp.bfloat16
F32 = jnp.float32


def send(value, ctx_count, fsdp_count, target):
    pairs = []
    for i in range(ctx_count):
        for j in range(fsdp_count):
            to = target(i, j)
            if to is not None:
                pairs.append((i * fsdp_count + j, to[0] * fsdp_count + to[1]))
    return lax.ppermute(value, AXES, pairs)


def after(values, *others):
    return lax.optimization_barrier((tuple(values), others))[0]


def near(*values):
    return [pltpu.with_memory_space_constraint(value, pltpu.VMEM) for value in values]


def split_high_low(value):
    high = value.astype(BF16)
    return high, (value - high.astype(F32)).astype(BF16)


def filter_body(
    decay_ref, residue_ref, decay_col_ref, residue_col_ref, taps_ref, skip_ref,
    near_ref, into_ref, outof_ref, step_ref, side_ref, rows_ref,
):
    side_ref[...] = jnp.broadcast_to(skip_ref[...], side_ref.shape)
    rows_ref[...] = taps_ref[...]
    groups, modes = decay_ref.shape
    rows = lax.broadcasted_iota(jnp.int32, (CHUNK, CHUNK), 0)
    cols = lax.broadcasted_iota(jnp.int32, (CHUNK, CHUNK), 1)
    lag = (cols - rows).astype(F32)
    clipped = jnp.maximum(lag, 0.0)
    back = (CHUNK - 1 - lax.broadcasted_iota(jnp.int32, (CHUNK, modes), 0)).astype(F32)
    ahead = (1 + lax.broadcasted_iota(jnp.int32, (modes, CHUNK), 1)).astype(F32)
    for group in range(groups):
        total = jnp.zeros((CHUNK, CHUNK), F32)
        for mode in range(modes):
            total += residue_ref[group, mode] * jnp.exp(-decay_ref[group, mode] * clipped)
        near_ref[group] = jnp.where(lag >= 0.0, total, 0.0).astype(BF16)
        rate_row = decay_col_ref[group, 0:1, :]
        into_high, into_low = split_high_low(jnp.exp(-rate_row * back))
        into_ref[group] = jnp.concatenate([into_high, into_low], axis=1)
        rate_col = jnp.swapaxes(jnp.broadcast_to(rate_row, (8, modes)), 0, 1)[:, 0:1]
        residue_row = residue_col_ref[group, 0:1, :]
        residue_col = jnp.swapaxes(jnp.broadcast_to(residue_row, (8, modes)), 0, 1)[:, 0:1]
        outof_high, outof_low = split_high_low(residue_col * jnp.exp(-rate_col * ahead))
        outof_ref[group] = jnp.concatenate([outof_high, outof_high, outof_low], axis=0)
        step_ref[group] = jnp.exp(-rate_row * CHUNK)


def make_filters(decay, residue, taps, skip):
    groups, modes = decay.shape
    smem = pl.BlockSpec(memory_space=pltpu.SMEM)
    vmem = pl.BlockSpec(memory_space=pltpu.VMEM)
    return pl.pallas_call(
        filter_body,
        in_specs=[smem, smem] + [vmem] * 4,
        out_specs=[vmem] * 6,
        out_shape=[
            jax.ShapeDtypeStruct((groups, CHUNK, CHUNK), BF16),
            jax.ShapeDtypeStruct((groups, CHUNK, 2 * modes), BF16),
            jax.ShapeDtypeStruct((groups, 3 * modes, CHUNK), BF16),
            jax.ShapeDtypeStruct((groups, 1, modes), F32),
            jax.ShapeDtypeStruct((skip.shape[0], 128), F32),
            jax.ShapeDtypeStruct(taps.shape, F32),
        ],
        name="filters",
    )(decay, residue, decay[:, None, :], residue[:, None, :], taps, skip)


def table_body(count, place_ref, own_ref, across_ref, beside_ref, gain_ref, *refs):
    raw_ref, scaled_ref, extra_ref, flip_ref = refs[-4:]
    weight_refs, token_refs, out_refs = refs[:count], refs[count:2 * count], refs[2 * count:-4]
    vocab, columns = own_ref.shape
    width = columns // count
    pieces, rows = len(out_refs), out_refs[0].shape[0]
    low_at, origin, high_at = place_ref[0], place_ref[1], place_ref[3]

    @pl.when(origin == 0)
    def _():
        raw_ref[...] = own_ref[...].astype(F32)

    @pl.when(origin == 1)
    def _():
        raw_ref[...] = across_ref[...].astype(F32)

    @pl.when(origin == 2)
    def _():
        raw_ref[...] = beside_ref[...].astype(F32)

    raw = raw_ref[...]
    scaled_ref[...] = (raw * gain_ref[:, pl.ds(pl.multiple_of(high_at * columns, columns), columns)]).astype(BF16)
    extra_ref[...] = jnp.zeros_like(extra_ref)
    squares = jnp.broadcast_to(jnp.sum(raw * raw, axis=1, keepdims=True), (vocab, 128))
    squares = jnp.swapaxes(squares, 0, 1)[0:1, :]
    for row in range(3):
        rounded = squares.astype(BF16).astype(F32)
        extra_ref[row:row + 1, :] = rounded
        squares = squares - rounded
    for shift, token_ref in enumerate(token_refs):
        low = lax.rem(low_at + shift, count)
        extra_ref[pl.ds(3 + low, 1), :] = (token_ref[...] // BASE).astype(F32)
        extra_ref[pl.ds(3 + count + low, 1), :] = (token_ref[...] % BASE).astype(F32)
    extra = extra_ref[...].astype(BF16)
    each = (rows - EXTRA) // 3
    for out_ref in out_refs:
        out_ref[:EXTRA, :] = extra
    for kind in range(3):
        total = None
        for shift, weight_ref in enumerate(weight_refs):
            start = pl.multiple_of(lax.rem(low_at + shift, count) * width, width)
            part = jnp.dot(scaled_ref[:, pl.ds(start, width)], weight_ref[kind], preferred_element_type=F32)
            total = part if total is None else total + part
        flip_ref[...] = jnp.swapaxes(total, 0, 1)
        for shift, out_ref in enumerate(out_refs):
            start = pl.multiple_of(lax.rem(high_at + shift, pieces) * each, each)
            out_ref[EXTRA + kind * each:EXTRA + (kind + 1) * each, :] = flip_ref[pl.ds(start, each), :].astype(BF16)


def make_table(place, own, across, beside, gain, weights, tokens, pieces):
    vocab = own.shape[0]
    channels = weights[0].shape[2]
    vmem = pl.BlockSpec(memory_space=pltpu.VMEM)
    return pl.pallas_call(
        functools.partial(table_body, len(weights)),
        in_specs=[pl.BlockSpec(memory_space=pltpu.SMEM)] + [vmem] * (4 + len(weights) + len(tokens)),
        out_specs=[vmem] * pieces,
        out_shape=[pltpu.VMEM((EXTRA + 3 * channels // pieces, vocab), BF16)] * pieces,
        scratch_shapes=[
            pltpu.VMEM(own.shape, F32),
            pltpu.VMEM(own.shape, BF16),
            pltpu.VMEM((EXTRA, vocab), F32),
            pltpu.VMEM((channels, vocab), F32),
        ],
        name="table",
    )(place, own, across, beside, gain, *weights, *tokens)


def mixer_body(width, taps, place_ref, near_ref, into_ref, outof_ref, step_ref, skip_ref, taps_ref, *refs):
    query_ref, drive_ref, conv_ref, token_ref, stage_ref, found_ref = refs[-6:]
    ctx_at = place_ref[2]
    out_refs = refs[-6 - token_ref.shape[0]:-6]
    piece_refs = refs[:-6 - token_ref.shape[0]]
    rows, vocab = piece_refs[0].shape
    rows -= EXTRA
    channels = rows // 3
    blocks, _, block = token_ref.shape
    length = blocks * block
    count = len(piece_refs)
    lows = blocks // count
    total = None
    squares = None
    for shift, ref in enumerate(piece_refs):
        head = ref[:EXTRA, :].astype(F32)
        summed = head[0:1] + head[1:2] + head[2:3]
        squares = summed if squares is None else squares + summed
        high = lax.rem(ctx_at // lows - shift + count, count)
        for low in range(lows):
            ids = head[3 + low:4 + low] * BASE + head[3 + lows + low:4 + lows + low]
            token_ref[high * lows + low] = ids[:, :block].astype(jnp.int32)
        part = ref[EXTRA:, :].astype(F32)
        total = part if total is None else total + part
    scaled = total * lax.rsqrt(squares * (1.0 / width) + 1e-05)
    half = found_ref.shape[3]
    laid = [scaled[:2 * channels], jnp.zeros((half - channels, vocab), F32), scaled[2 * channels:]]
    if half > 2 * channels:
        laid.append(jnp.zeros((half - 2 * channels, vocab), F32))
    table = jnp.swapaxes(jnp.concatenate(laid, axis=0), 0, 1).astype(BF16)
    ids = lax.broadcasted_iota(jnp.int32, (TILE, vocab), 1)
    is_query = lax.broadcasted_iota(jnp.int32, (STRIP, half), 1) < channels

    for tile in range(length // TILE):
        at = tile * TILE
        inside = at % block
        tokens = jnp.swapaxes(
            jnp.broadcast_to(token_ref[at // block][:, inside:inside + TILE], (128, TILE)), 0, 1
        )
        hot = jnp.where(ids == jnp.concatenate([tokens] * (vocab // 128), axis=1), 1.0, 0.0).astype(BF16)
        here_ref = found_ref.at[tile % 2]
        found = jnp.dot(hot, table, preferred_element_type=F32)
        for side in range(2):
            if tile == 0:
                here_ref[side, :8] = jnp.zeros((8, half), F32)
            else:
                here_ref[side, :8] = found_ref[(tile - 1) % 2, side, TILE:]
            here_ref[side, 8:] = found[:, side * half:(side + 1) * half]
        for strip in range(0, TILE, STRIP):
            sums = []
            for side in range(2):
                lanes = slice(side * half, (side + 1) * half)
                total = None
                for lag in range(taps):
                    first = 8 - lag + strip
                    term = taps_ref[lag:lag + 1, lanes] * here_ref[side, first:first + STRIP, :]
                    total = term if total is None else total + term
                sums.append(total)
            both = jnp.where(is_query, sums[0], sums[0] * sums[1])
            flat = jnp.swapaxes(both, 0, 1)
            query_ref[:, at + strip:at + strip + STRIP] = flat[:channels]
            drive_ref[:, at + strip:at + strip + STRIP] = flat[channels:2 * channels]
    groups = near_ref.shape[0]
    per = channels // groups
    modes = step_ref.shape[2]
    chunks = length // CHUNK
    for group in range(groups):
        base = group * per
        stacked = jnp.concatenate(
            [drive_ref[base:base + per, n * CHUNK:(n + 1) * CHUNK] for n in range(chunks)], axis=0
        ).astype(BF16)
        both = jnp.dot(stacked, into_ref[group], preferred_element_type=F32)
        ends = both[:, :modes] + both[:, modes:]
        step = step_ref[group]
        state = jnp.zeros((per, modes), F32)
        starts = []
        for n in range(chunks):
            starts.append(state)
            state = state * step + ends[n * per:(n + 1) * per]
        high, low = split_high_low(jnp.concatenate(starts, axis=0))
        conv_ref[...] = jnp.dot(stacked, near_ref[group], preferred_element_type=F32) + jnp.dot(
            jnp.concatenate([high, low, high], axis=1), outof_ref[group], preferred_element_type=F32
        )
        for n in range(chunks):
            here = slice(n * CHUNK, (n + 1) * CHUNK)
            response = conv_ref[n * per:(n + 1) * per, :] + jnp.concatenate([skip_ref[base:base + per, :]] * (CHUNK // 128), axis=1) * drive_ref[base:base + per, here]
            at = n * CHUNK
            stage_ref[at // block, base:base + per, at % block:at % block + CHUNK] = (
                query_ref[base:base + per, here] * response
            ).astype(BF16)
    for shift, out_ref in enumerate(out_refs):
        out_ref[...] = stage_ref[lax.rem(ctx_at + shift, blocks)]


def make_mixer(place, width, taps, block, filters, pieces, blocks):
    rows = pieces[0].shape[0] - EXTRA
    channels = rows // 3
    length = block * blocks
    groups = filters[0].shape[0]
    vmem = pl.BlockSpec(memory_space=pltpu.VMEM)
    return pl.pallas_call(
        functools.partial(mixer_body, width, taps),
        in_specs=[pl.BlockSpec(memory_space=pltpu.SMEM)] + [vmem] * (6 + len(pieces)),
        out_specs=[vmem] * blocks,
        out_shape=[pltpu.VMEM((channels, block), BF16)] * blocks,
        scratch_shapes=[
            pltpu.VMEM((channels, length), F32),
            pltpu.VMEM((channels, length), F32),
            pltpu.VMEM((length // CHUNK * (channels // groups), CHUNK), F32),
            pltpu.VMEM((blocks, 1, block), jnp.int32),
            pltpu.VMEM((blocks, channels, block), BF16),
            pltpu.VMEM((2, 2, TILE + 8, filters[5].shape[1] // 2), F32),
        ],
        name="mixer",
    )(place, *filters, *near(*pieces))


def order_body(lows, place_ref, *refs):
    piece_refs, out_ref, stage_ref = refs[:-2], refs[-2], refs[-1]
    count = len(piece_refs)
    rows = piece_refs[0].shape[0]
    for shift, ref in enumerate(piece_refs):
        source = lax.rem(place_ref[2] - shift + count, count)
        start = pl.multiple_of((lax.rem(source, lows) * (count // lows) + source // lows) * rows, rows)
        stage_ref[pl.ds(start, rows), :] = ref[...].astype(F32)
    out_ref[...] = jnp.swapaxes(stage_ref[...], 0, 1).astype(BF16)


def make_order(place, pieces, lows):
    rows, length = pieces[0].shape
    vmem = pl.BlockSpec(memory_space=pltpu.VMEM)
    return pl.pallas_call(
        functools.partial(order_body, lows),
        in_specs=[pl.BlockSpec(memory_space=pltpu.SMEM)] + [vmem] * len(pieces),
        out_specs=vmem,
        out_shape=pltpu.VMEM((length, rows * len(pieces)), BF16),
        scratch_shapes=[pltpu.VMEM((rows * len(pieces), length), F32)],
        name="order",
    )(place, *near(*pieces))


def product_body(order, place_ref, *refs):
    side_refs = refs[:len(order)]
    out_ref, sides_ref, wide_ref, arrived = refs[-4:]
    block_refs = refs[len(order):-4]
    count = len(block_refs)
    full, cols = block_refs[0].shape
    copies = []
    for at, ref in enumerate(block_refs):
        first = full // 2 if at == count - 1 else 0
        start = pl.multiple_of(place_ref[PLACES + at] * full + first, full // 2)
        copies.append(
            pltpu.make_async_copy(
                ref,
                wide_ref.at[place_ref[PLACES + count + at], pl.ds(start, ref.shape[0])],
                arrived.at[at],
            )
        )
        copies[-1].start()
    for flip, ref in zip(order, side_refs):
        sides_ref[:, flip * full:(flip + 1) * full] = ref[...]
    for copy in copies:
        copy.wait()
    for low in range(wide_ref.shape[0]):
        out_ref[:, low * cols:(low + 1) * cols] = jnp.dot(
            sides_ref[...], wide_ref[low], preferred_element_type=F32
        ).astype(BF16)


def make_product(place, order, sides, blocks, lows):
    length, full = sides[0].shape
    cols = blocks[0].shape[1]
    rows = blocks[0].shape[0]
    vmem = pl.BlockSpec(memory_space=pltpu.VMEM)
    return pl.pallas_call(
        functools.partial(product_body, order),
        in_specs=[pl.BlockSpec(memory_space=pltpu.SMEM)]
        + [vmem] * len(sides)
        + [pl.BlockSpec(memory_space=pl.ANY)] * len(blocks),
        out_specs=vmem,
        out_shape=jax.ShapeDtypeStruct((length, lows * cols), BF16),
        scratch_shapes=[
            pltpu.VMEM((length, len(sides) * full), BF16),
            pltpu.VMEM((lows, len(sides) * rows, cols), BF16),
            pltpu.SemaphoreType.DMA((len(blocks),)),
        ],
        name="product",
    )(place, *near(*sides), *blocks)


def reverse_bits(value, count):
    result = 0
    while count > 1:
        result, value, count = result * 2 + value % 2, value // 2, count // 2
    return result


def cycle_of(highs, lows):
    walk = [(high, 0) for high in range(highs)]
    for at in range(highs - 1, -1, -1):
        lows_at = range(1, lows) if (highs - 1 - at) % 2 == 0 else range(lows - 1, 0, -1)
        walk += [(at, low) for low in lows_at]
    return [high * lows + low for high, low in walk]


def body(
    tokens,
    embedding,
    norm_gain,
    in_weight,
    short_taps,
    decay_rates,
    residue,
    skip_weight,
    out_weight,
):
    ctx_count = lax.axis_size("ctx")
    fsdp_count = lax.axis_size("fsdp")
    lows = ctx_count // fsdp_count
    ctx_at = lax.axis_index("ctx")
    fsdp_at = lax.axis_index("fsdp")
    high_at, low_at = ctx_at // lows, ctx_at % lows
    tok_count = tokens.shape[0]
    _, columns = embedding.shape
    local_channels = in_weight.shape[2]
    part = local_channels // lows
    own = local_channels // ctx_count

    def move(value, target):
        return send(value, ctx_count, fsdp_count, target)

    by_kind = jnp.swapaxes(in_weight, 0, 1)
    weights, ids = [], [tokens[None, :]]
    for shift in range(1, lows):
        def neighbour(i, j):
            return (i // lows * lows + (i % lows - shift) % lows, j)

        going = lax.dynamic_slice_in_dim(by_kind, (low_at - shift) % lows * part, part, 2)
        weights.append(move(going, neighbour))
        ids.append(move(tokens[None, :], neighbour))

    weights.insert(0, lax.dynamic_slice_in_dim(by_kind, low_at * part, part, 2))

    chips = fsdp_count // 2
    across = None
    for shift in range(1, chips):
        got = move(
            embedding, lambda i, j: (i, (j + 2 * shift) % fsdp_count) if j == i // lows else None
        )
        across = got if across is None else across + got
    cycle = cycle_of(fsdp_count, lows)
    spot = {ctx: at for at, ctx in enumerate(cycle)}
    moved = move(
        out_weight,
        lambda i, j: ((reverse_bits(j, fsdp_count) ^ i // lows) * lows + i % lows, i // lows),
    )
    ahead, behind = [moved], [moved]
    rounds = (ctx_count - 1) // 2
    steps = [*range(rounds + 1), *range(-1, -rounds - 1, -1), rounds + 1, rounds + 1]
    known = []
    for i in range(ctx_count):
        met = [cycle[(spot[i] - step) % ctx_count] for step in steps]
        for j in range(fsdp_count):
            origin = 0 if j == i // lows else 1 if (j - i // lows) % 2 == 0 else 2
            flips = [reverse_bits(ctx // lows ^ j, fsdp_count) ^ j for ctx in met]
            known.append([i % lows, origin, i, i // lows, *flips, *(ctx % lows for ctx in met)])
    place = jnp.array(known, jnp.int32)[ctx_at * fsdp_count + fsdp_at]

    gain = norm_gain[None, :]
    (across,) = after((across,), place)
    holder = jnp.where(fsdp_at == high_at, embedding, across)
    beside = move(holder, lambda i, j: (i, j ^ 1) if j % 2 == i // lows % 2 else None)

    def turn(*others):
        low, high = after((ahead[-1], behind[-1]), *others)
        ahead.append(move(low, lambda i, j: (cycle[(spot[i] + 1) % ctx_count], j)))
        behind.append(move(high, lambda i, j: (cycle[(spot[i] - 1) % ctx_count], j)))

    turn()
    outgoing = make_table(place, embedding, across, beside, gain, weights, ids, fsdp_count)
    pieces = [outgoing[0]]
    for shift in range(1, fsdp_count):
        pieces.append(
            move(outgoing[shift], lambda i, j: ((i // lows + shift) % fsdp_count * lows + i % lows, j))
        )

    decay_rates, residue, short_taps, skip_weight = after(
        (decay_rates, residue, short_taps, skip_weight), *outgoing
    )
    channel_at = low_at * part + high_at * own
    per_group = min(GROUP, own)
    group_count = own // per_group
    decay = lax.dynamic_slice_in_dim(decay_rates.T, channel_at // GROUP, group_count, 0)
    weight = lax.dynamic_slice_in_dim(residue.T, channel_at // GROUP, group_count, 0)
    taps = lax.dynamic_slice_in_dim(short_taps, channel_at, own, 2)
    lanes = -(-2 * own // 128) * 128
    taps = jnp.concatenate(
        [
            jnp.pad(taps[:, :2].reshape(-1, 2 * own), ((0, 0), (0, lanes - 2 * own))),
            jnp.pad(taps[:, 2], ((0, 0), (own, lanes - 2 * own))),
        ],
        axis=1,
    )
    skip = lax.dynamic_slice_in_dim(skip_weight, channel_at, own, 0)[:, None]
    filters = make_filters(decay, weight, taps, skip)
    for _ in range(1, rounds - 1):
        turn(filters[-1])
    gated = make_mixer(
        place, columns * fsdp_count, short_taps.shape[0], tok_count, filters, pieces, ctx_count
    )

    pieces = [gated[0]]
    for shift in range(1, ctx_count):
        pieces.append(move(gated[shift], lambda i, j: ((i + shift) % ctx_count, j)))
    pieces = list(after(pieces, ahead[-1], behind[-1]))
    turn(gated[0])
    ordered = make_order(place, pieces, lows)
    middle = out_weight.shape[0] // 2
    low, high = after((ahead[-1], behind[-1]), ordered)
    last_ahead = move(low[:middle], lambda i, j: (cycle[(spot[i] + 1) % ctx_count], j))
    last_behind = move(high[middle:], lambda i, j: (cycle[(spot[i] - 1) % ctx_count], j))
    blocks = ahead + behind[1:] + [last_ahead, last_behind]
    sides, order = [ordered], [0]
    reach = fsdp_count // 2
    while reach:
        more = []
        for side in sides:
            more.append(move(side, lambda i, j: (i, j ^ reach)))
        sides = sides + more
        order = order + [at ^ reach for at in order]
        reach //= 2
    return make_product(place, tuple(order), sides, blocks, lows)


def solution(mesh):
    placed = (
        P("ctx"),
        P(None, "fsdp"),
        P(),
        P("ctx", None, "fsdp"),
        P(None, None, "fsdp"),
        P(None, "fsdp"),
        P(None, "fsdp"),
        P("fsdp"),
        P("fsdp", "ctx"),
    )
    return jax.shard_map(body, mesh=mesh, in_specs=placed, out_specs=P("ctx", "fsdp"), check_vma=False)
```
